512 devices in a mesh: tile: 128 (over y, z_hi, x, core), grp: 4 (over z_lo).
Axes of the slice: x: 4, y: 4, z: 16 (z_hi: 4, z_lo: 4; z = z_hi * 4 + z_lo), core: 2. Of those that a mesh axis runs over, the one named last changes fastest.
Arguments:
- forcing_vector: float32 [70, 1024, 512], P(None, 'tile', 'grp'), may hold values from -8 to 8
- shift_weights: float32 [70, 1024, 512], P(None, 'tile', 'grp'), may hold values from 0.0001 to 0.0004
- layer_link_factor: float32 [69], replicated, may hold values from 0.5 to 8
- previous_kelvin_field: float32 [70, 8, 65536], P(None, None, ('tile', 'grp')), may hold values from 0.8 to 1.2
- longwave_opacity: float32 [70], replicated, may hold values from 0.02 to 0.5
- shortwave_opacity: float32 [70], replicated, may hold values from 0.01 to 0.05
Outputs:
- solution_field: float32 [70, 1024, 512], P(None, 'tile', 'grp')
- radiation_state: float32 [70, 8, 65536], P(None, None, ('tile', 'grp'))
The draws below stay inside these ranges and needn't reach their ends.
All inputs are finite; a program needn't handle non-finite values.
Results may differ from the reference program's by a relative error of at most 0.0003.
Values sent between devices are 32-bit elements; how exact they have to be, the bound alone decides.
A program may use at most 64 MiB of HBM per device.

```python
import math
import jax
import jax.numpy as jnp
from jax import lax

LAYER_TOTAL = 70
SHARD_POINTS = 8
CY = 128
ITERS = 2
STRIP_POINTS = 1024
SPAN_POINTS = 512
N_TILE = 128
N_GRP = 4


def block_scale(rng, dims, shards, least, high):
    factor_of, own = 1.0, jax.random.fold_in(rng, 6)
    for axis_at, blocks in shards:
        draws = jnp.exp(jax.random.uniform(jax.random.fold_in(own, axis_at), (blocks,), jnp.float32, least / len(shards), high / len(shards)))
        factor_of = factor_of * jnp.repeat(draws, dims[axis_at] // blocks).reshape([-1 if axis == axis_at else 1 for axis in range(len(dims))])
    return factor_of


def noise(key, dims, scale, reach, split=(), kind=jnp.bfloat16):
    array = jax.random.normal(key, dims, jnp.float32) * scale
    if len(split) > 0:
        array = block_scale(key, dims, split, -0.22, 0.18) * array
    return jnp.clip(array, min=-reach, max=reach).astype(kind)


def setup_inputs(seed: int = 0) -> dict:
    splits = jax.random.split(jax.random.key(seed), 7)
    return {
        "forcing_vector": noise(splits[0], (LAYER_TOTAL, STRIP_POINTS, SPAN_POINTS), 1.0, 8.0, ((1, 128), (2, 4)), jnp.float32),
        "shift_weights": jnp.clip(jnp.exp(math.log(0.0004) - 1.3862944 * jax.random.uniform(splits[1], (LAYER_TOTAL, STRIP_POINTS, SPAN_POINTS), jnp.float32) ** block_scale(splits[1], (LAYER_TOTAL, STRIP_POINTS, SPAN_POINTS), ((1, 128), (2, 4)), -0.2, 0.2)), 0.0001, 0.0004),
        "layer_link_factor": jnp.clip(jnp.exp(jax.random.uniform(splits[2], (LAYER_TOTAL - 1,), jnp.float32, math.log(0.5), math.log(8.0))), 0.5, 8.0),
        "previous_kelvin_field": jnp.clip(0.8 + 0.40000004 * jax.random.uniform(splits[3], (LAYER_TOTAL, SHARD_POINTS, STRIP_POINTS // SHARD_POINTS * SPAN_POINTS), jnp.float32) ** block_scale(splits[3], (LAYER_TOTAL, SHARD_POINTS, STRIP_POINTS // SHARD_POINTS * SPAN_POINTS), ((2, 512),), -0.2, 0.2), 0.8, 1.2),
        "longwave_opacity": jnp.clip(jnp.exp(jax.random.uniform(splits[4], (LAYER_TOTAL,), jnp.float32, math.log(0.02), math.log(0.5))), 0.02, 0.5),
        "shortwave_opacity": jnp.clip(jnp.exp(jax.random.uniform(splits[5], (LAYER_TOTAL,), jnp.float32, math.log(0.01), math.log(0.05))), 0.01, 0.05),
    }


def column_inverse(layer_link_factor):
    size = layer_link_factor.shape[0] + 1
    zero_one = jnp.zeros((1,), jnp.float32)
    upper = jnp.concatenate([layer_link_factor, zero_one])
    lower = jnp.concatenate([zero_one, layer_link_factor])
    matrix = jnp.diag(4.0 + upper + lower) - jnp.diag(layer_link_factor, 1) - jnp.diag(layer_link_factor, -1)
    factor = jnp.linalg.cholesky(matrix)
    return jax.scipy.linalg.cho_solve((factor, True), jnp.eye(size, dtype=jnp.float32))

def radiation_tables(longwave_opacity, shortwave_opacity):
    levels = longwave_opacity.shape[0]
    transmitted = jnp.exp(-longwave_opacity)
    zero_one = jnp.zeros((1,), jnp.float32)
    interfaces = jnp.concatenate([zero_one, jnp.cumsum(longwave_opacity)])
    interface_index = jnp.arange(levels + 1)[:, None]
    layer_index = jnp.arange(levels)[None, :]
    below_mask = layer_index < interface_index
    gap_down = jnp.where(below_mask, interfaces[:, None] - interfaces[None, 1:], 0.0)
    downward = jnp.where(below_mask, jnp.exp(-gap_down), 0.0) * (1.0 - transmitted)[None, :]
    above_mask = layer_index >= interface_index
    gap_up = jnp.where(above_mask, interfaces[None, :-1] - interfaces[:, None], 0.0)
    upward = jnp.where(above_mask, jnp.exp(-gap_up), 0.0) * (1.0 - transmitted)[None, :]
    surface = jnp.exp(-(interfaces[-1] - interfaces))
    upward = upward.at[:, levels - 1].add(surface)
    matrix = downward[:-1] - downward[1:] + upward[1:] - upward[:-1]
    solar_edges = jnp.concatenate([zero_one, jnp.cumsum(shortwave_opacity)])
    absorbed = 10.0 * (jnp.exp(-solar_edges[:-1]) - jnp.exp(-solar_edges[1:]))
    return (matrix, absorbed)

def sun_cosine(global_row, total_rows):
    latitude = ((global_row.astype(jnp.float32) + 0.5) / total_rows - 0.5) * (math.pi / 2)
    return jnp.cos(latitude - 0.4)

def vertical(source, layer_link_factor):
    fluxes = layer_link_factor[:, None, None] * (source[:-1] - source[1:])
    zeros_level = jnp.zeros_like(source[:1])
    return jnp.concatenate([fluxes, zeros_level], axis=0) - jnp.concatenate([zeros_level, fluxes], axis=0)

def operate(source, shift_weights, layer_link_factor):
    western = jnp.roll(source, 1, axis=1)
    eastern = jnp.roll(source, -1, axis=1)
    padded = jnp.concatenate([source[:, :, :1], source, source[:, :, -1:]], axis=2)
    beside = western + eastern + padded[:, :, 2:] + padded[:, :, :-2]
    return shift_weights * source + 4.0 * source - beside + vertical(source, layer_link_factor)

def coarse_matrix(block_mass, tile_count, group_count):
    block_count = tile_count * group_count
    ordering = jnp.arange(block_count)
    tile_of = ordering // group_count
    group_of = ordering % group_count
    same_group = group_of[:, None] == group_of[None, :]
    tile_gap = (tile_of[:, None] - tile_of[None, :]) % tile_count
    x_near = same_group & ((tile_gap == 1) | (tile_gap == tile_count - 1))
    same_tile = tile_of[:, None] == tile_of[None, :]
    y_near = (same_tile & (jnp.abs(group_of[:, None] - group_of[None, :]) == 1)).astype(jnp.float32)
    y_count = jnp.sum(y_near, axis=1)
    diagonal = block_mass + 2.0 * LAYER_TOTAL * CY + LAYER_TOTAL * SHARD_POINTS * y_count
    return jnp.diag(diagonal) - LAYER_TOTAL * CY * x_near.astype(jnp.float32) - LAYER_TOTAL * SHARD_POINTS * y_near

def radiation_layout(full):
    share_rows = CY // N_TILE
    shaped = full.reshape(LAYER_TOTAL, N_TILE, SHARD_POINTS, N_GRP, N_TILE, share_rows)
    return shaped.transpose(0, 2, 4, 3, 1, 5).reshape(LAYER_TOTAL, SHARD_POINTS, N_TILE * N_GRP * CY)

def grid_layout(columns):
    share_rows = CY // N_TILE
    shaped = columns.reshape(LAYER_TOTAL, SHARD_POINTS, N_TILE, N_GRP, N_TILE, share_rows)
    return shaped.transpose(0, 4, 1, 3, 2, 5).reshape(LAYER_TOTAL, N_TILE * SHARD_POINTS, N_GRP * CY)

def reference(forcing_vector, shift_weights, layer_link_factor, previous_kelvin_field, longwave_opacity, shortwave_opacity):
    highest = lax.Precision.HIGHEST
    matrix, absorbed = radiation_tables(longwave_opacity, shortwave_opacity)
    share_rows = CY // N_TILE
    position = jnp.arange(N_TILE * N_GRP * CY)
    block_index = position // CY
    inside = position % CY
    device_tile = block_index // N_GRP
    device_group = block_index % N_GRP
    global_row = device_group * CY + device_tile * share_rows + inside % share_rows
    cosine = sun_cosine(global_row, N_GRP * CY)
    second_power_entry = previous_kelvin_field * previous_kelvin_field
    emission = second_power_entry * second_power_entry
    column_heating = jnp.dot(matrix, emission.reshape(LAYER_TOTAL, -1), precision=highest).reshape(emission.shape)
    column_heating = column_heating + absorbed[:, None, None] * cosine[None, None, :]
    column_heating = column_heating - jnp.mean(column_heating, axis=0, keepdims=True)
    forcing = forcing_vector + grid_layout(column_heating)
    inverse = column_inverse(layer_link_factor)
    block_mass = shift_weights.reshape(LAYER_TOTAL, N_TILE, SHARD_POINTS, N_GRP, CY).sum(axis=(0, 2, 4)).reshape(-1)
    factor = jnp.linalg.cholesky(coarse_matrix(block_mass, N_TILE, N_GRP))
    solution = jnp.zeros_like(forcing)
    residual = forcing
    directions = []
    images = []
    image_norms = []
    for number in range(ITERS):
        smooth = jnp.dot(inverse, residual.reshape(LAYER_TOTAL, -1), precision=highest).reshape(residual.shape)
        remainder = residual - operate(smooth, shift_weights, layer_link_factor)
        block_sums = remainder.reshape(LAYER_TOTAL, N_TILE, SHARD_POINTS, N_GRP, CY).sum(axis=(0, 2, 4)).reshape(-1)
        coarse = jax.scipy.linalg.cho_solve((factor, True), block_sums)
        spread = jnp.repeat(jnp.repeat(coarse.reshape(N_TILE, N_GRP), SHARD_POINTS, axis=0), CY, axis=1)
        direction = smooth + spread[None]
        operator_image = operate(direction, shift_weights, layer_link_factor)
        weights = [jnp.sum(operator_image * earlier) / norm_value for earlier, norm_value in zip(images, image_norms)]
        for weight, earlier_direction, earlier_image in zip(weights, directions, images):
            direction = direction - weight * earlier_direction
            operator_image = operator_image - weight * earlier_image
        image_norm = jnp.sum(operator_image * operator_image)
        step_size = jnp.sum(residual * operator_image) / image_norm
        solution = solution + step_size * direction
        residual = residual - step_size * operator_image
        directions.append(direction)
        images.append(operator_image)
        image_norms.append(image_norm)
    return (solution, radiation_layout(solution))
```

```python
import math

import jax
import jax.numpy as jnp
from jax import lax
from jax.experimental import pallas as pl
from jax.experimental.pallas import tpu as pltpu
from jax.sharding import PartitionSpec as P

LV = 70
PX = 8
CY = 128
NG = 4
DIMS = (4, 4, 4, 2)
NT = 128
LP = 80
NCH = LP // 16
UNROLL = 10
NM = 16
GP = 8
F32 = jnp.float32
MESH = pl.DeviceIdType.MESH


def iota(shape, dim):
    return lax.broadcasted_iota(jnp.int32, shape, dim)


def roll(value, shift, axis):
    return pltpu.roll(value, shift, axis)


def blocked(levels, body, init, reverse=False):
    def trip(b, carry):
        for j in range(UNROLL):
            k = b * UNROLL + j
            carry = body(levels - 1 - k if reverse else k, carry)
        return carry

    return lax.fori_loop(0, levels // UNROLL, trip, init)


def total(value):
    return jnp.sum(jnp.sum(value, axis=0, keepdims=True), axis=1, keepdims=True)


def matmul4(left, right):
    out = []
    for j in range(NG):
        term = left[0] * right[j][0:1, :]
        for l in range(1, NG):
            term = term + left[l] * right[j][l : l + 1, :]
        out.append(term)
    return out


def inverse4(columns):
    columns = list(columns)
    row = iota((GP, NT), 0)
    for k in range(NG):
        pivot = 1.0 / columns[k][k : k + 1, :]
        for j in range(NG):
            if j != k:
                scaled = columns[j][k : k + 1, :] * pivot
                columns[j] = jnp.where(row == k, scaled, columns[j] - columns[k] * scaled)
        columns[k] = jnp.where(row == k, pivot, -columns[k] * pivot)
    return columns


def matvec4(columns, vector):
    out = columns[0] * vector[0:1, :]
    for l in range(1, NG):
        out = out + columns[l] * vector[l : l + 1, :]
    return out


def kernel(
    fv,
    sh,
    kel,
    link,
    longwave,
    shortwave,
    out_field,
    out_rad,
    down,
    upw,
    lco,
    cco,
    res,
    smooth0,
    smooth1,
    image,
    hs,
    hr,
    xs,
    xr,
    west_send,
    east_send,
    south_send,
    north_send,
    west_recv,
    east_recv,
    south_recv,
    north_recv,
    zbuf,
    pbuf,
    alpha_co,
    gamma_co,
    last_co,
    line_count,
    row_count,
    a2a_send_sem,
    a2a_recv_sem,
    halo_send_sem,
    halo_recv_sem,
    z_send_sem,
    z_recv_sem,
    p_send_sem,
    p_recv_sem,
):
    ny, nzh, nx, nc = DIMS
    nz = nzh * NG
    np_ = ny * nx * nc
    t = lax.axis_index("tile")
    g = lax.axis_index("grp")
    c = lax.rem(t, nc)
    x = lax.rem(lax.div(t, nc), nx)
    zh = lax.rem(lax.div(t, nc * nx), nzh)
    y = lax.div(t, nc * nx * nzh)
    z = zh * NG + g
    p = (y * nx + x) * nc + c

    def tile_of(y_, zh_, x_, c_):
        return ((y_ * nzh + zh_) * nx + x_) * nc + c_

    def a2a_peer(j):
        dz = lax.rem(j, nzh)
        rest = lax.div(j, nzh)
        dc = lax.rem(rest, nc)
        rest = lax.div(rest, nc)
        dx = lax.rem(rest, nx)
        dy = lax.div(rest, nx)
        return tile_of(
            lax.rem(y + dy, ny), lax.rem(zh + dz, nzh), lax.rem(x + dx, nx), lax.rem(c + dc, nc)
        )

    def z_peer(k):
        z2 = lax.rem(z + k, nz)
        return tile_of(y, lax.div(z2, NG), x, c), lax.rem(z2, NG)

    def p_peer(k):
        p2 = lax.rem(p + k, np_)
        return tile_of(lax.div(p2, nx * nc), zh, lax.rem(lax.div(p2, nc), nx), lax.rem(p2, nc))

    barrier = pltpu.get_barrier_semaphore()

    def greet_tile(j, _):
        pl.semaphore_signal(barrier, inc=1, device_id=(a2a_peer(j), g), device_id_type=MESH)
        return 0

    def greet_grp(j, _):
        dzh = lax.rem(j, nzh)
        dg = lax.div(j, nzh) + 1
        pl.semaphore_signal(
            barrier,
            inc=1,
            device_id=(tile_of(y, lax.rem(zh + dzh, nzh), x, c), lax.rem(g + dg, NG)),
            device_id_type=MESH,
        )
        return 0

    lax.fori_loop(1, NT, greet_tile, 0)
    lax.fori_loop(0, (NG - 1) * nzh, greet_grp, 0)

    def wait_lines(sem):
        pltpu.make_async_copy(line_count, line_count, sem).wait()

    def wait_rows(sem):
        rows = row_count.at[pl.ds(0, nz - 1)]
        pltpu.make_async_copy(rows, rows, sem).wait()

    def a2a_start(src, dst, which):
        def send(j, _):
            peer = a2a_peer(j)
            pltpu.make_async_remote_copy(
                src_ref=src.at[pl.ds(peer, 1), :],
                dst_ref=dst.at[pl.ds(t, 1), :],
                send_sem=a2a_send_sem.at[which],
                recv_sem=a2a_recv_sem.at[which],
                device_id=(peer, g),
                device_id_type=MESH,
            ).start()
            return 0

        lax.fori_loop(1, NT, send, 0)

    def a2a_wait(which):
        wait_lines(a2a_recv_sem.at[which])

    def a2a_drain(which):
        wait_lines(a2a_send_sem.at[which])

    lane = iota((PX, CY), 1)
    row8 = iota((PX, CY), 0)

    def pack_row(values):
        rows = [jnp.sum(v, axis=0, keepdims=True) for v in values]
        rows = rows + [jnp.zeros((1, CY), F32)] * (NM - len(rows))
        sums = jnp.sum(jnp.concatenate(rows, axis=0), axis=1, keepdims=True)
        diag = iota((NM, 128), 0) == iota((NM, 128), 1)
        return jnp.sum(jnp.where(diag, sums, 0.0), axis=0, keepdims=True)

    def gather_start(which, row):
        buf = zbuf.at[which]
        buf[pl.ds(z, 1), :] = row

        def send(k, _):
            pltpu.make_async_remote_copy(
                src_ref=buf.at[pl.ds(z, 1), :],
                dst_ref=buf.at[pl.ds(z, 1), :],
                send_sem=z_send_sem.at[which],
                recv_sem=z_recv_sem.at[which],
                device_id=z_peer(k),
                device_id_type=MESH,
            ).start()
            return 0

        lax.fori_loop(1, nz, send, 0)

    def gather_middle(which):
        buf = zbuf.at[which]
        wait_rows(z_recv_sem.at[which])
        value = buf[...]
        ln = iota((nz, 128), 1)
        mine = lax.rem(ln, nz) == iota((nz, 128), 0)
        packed = []
        for r in range(NM // 8):
            spread = jnp.take_along_axis(value, lax.rem(r * 8 + lax.div(ln, nz), 128), axis=1)
            packed.append(jnp.sum(jnp.where(mine, spread, 0.0), axis=0, keepdims=True))
        pbuf[which, pl.ds(p, 1)] = jnp.concatenate(packed, axis=0)[None]
        dst = pbuf.at[which]

        def send(k, _):
            pltpu.make_async_remote_copy(
                src_ref=dst.at[pl.ds(p, 1)],
                dst_ref=dst.at[pl.ds(p, 1)],
                send_sem=p_send_sem.at[which],
                recv_sem=p_recv_sem.at[which],
                device_id=(p_peer(k), g),
                device_id_type=MESH,
            ).start()
            return 0

        lax.fori_loop(1, np_, send, 0)

    def gather_end(which, count):
        rows = pbuf.at[which, pl.ds(0, np_ - 1)]
        pltpu.make_async_copy(rows, rows, p_recv_sem.at[which]).wait()
        parts = [pbuf[which, :, r, :] for r in range(NM // 8)]
        parts.append(jnp.zeros((128 - np_ * (NM // 8), 128), F32))
        flat = jnp.concatenate(parts, axis=0).T
        ln = iota((128, 128), 1)
        rw = iota((128, 128), 0)
        t_p = (lax.rem(lax.div(ln, nc * nx * nzh), ny) * nx * nc) + lax.rem(ln, nx * nc)
        t_zh = lax.rem(lax.div(ln, nc * nx), nzh)
        keep = lax.div(lax.rem(rw, nz), NG) == t_zh
        found = []
        for r in range(NM // 8):
            if len(found) >= count:
                break
            got = jnp.take_along_axis(flat, t_p + r * np_, axis=1)
            got = jnp.where(keep, got, 0.0)
            for m in range(8):
                if len(found) >= count:
                    break
                block = got[m * nz : (m + 1) * nz, :NT]
                acc = block[0:NG]
                for b in range(1, nzh):
                    acc = acc + block[b * NG : (b + 1) * NG]
                found.append(jnp.concatenate([acc, jnp.zeros((GP - NG, NT), F32)], axis=0))
        return found

    def gather_drain(which):
        wait_rows(z_send_sem.at[which])
        rows = pbuf.at[which, pl.ds(0, np_ - 1)]
        pltpu.make_async_copy(rows, rows, p_send_sem.at[which]).wait()

    zeros = jnp.zeros((PX, CY), F32)
    latitude = ((g * CY + t).astype(F32) + 0.5) / float(CY * NG) - 0.5
    mu10 = 10.0 * jnp.cos(jnp.full((PX, CY), latitude * (math.pi / 2) - 0.4, F32))

    def emission(k):
        square = kel[k] * kel[k]
        return square * square

    def both_passes(k, carry):
        flux_down, flux_up, sun, acc = carry
        em = emission(k)
        trans = jnp.exp(jnp.full((PX, CY), -longwave[k], F32))
        absorbed = 1.0 - trans
        sun_trans = jnp.exp(jnp.full((PX, CY), -shortwave[k], F32))
        raw = absorbed * (flux_down - 2.0 * em) + mu10 * (sun * (1.0 - sun_trans))
        down[k] = raw
        flux_down = trans * flux_down + absorbed * em
        sun = sun * sun_trans
        k2 = LV - 1 - k
        em2 = emission(k2)
        trans2 = jnp.exp(jnp.full((PX, CY), -longwave[k2], F32))
        absorbed2 = 1.0 - trans2
        raw2 = absorbed2 * flux_up
        upw[k2] = raw2
        flux_up = trans2 * flux_up + absorbed2 * em2
        return flux_down, flux_up, sun, acc + (raw + raw2)

    carry = blocked(LV, both_passes, (zeros, emission(LV - 1), jnp.ones((PX, CY), F32), zeros))
    mean = carry[3] * (1.0 / LV)
    for k in range(LV, LP):
        down[k] = zeros
        upw[k] = zeros
        res[k] = zeros
    for ch in range(NCH):
        lv = slice(ch * 16, (ch + 1) * 16)
        heat = down[lv] + upw[lv] - mean[None]
        hs[:, ch * 128 : (ch + 1) * 128] = heat.reshape(16 * PX, CY).T

    def factor(k, carry):
        link_above, inv_above = carry
        here = jnp.where(k < LV - 1, link[jnp.minimum(k, LV - 2)], 0.0)
        here = jnp.full((PX, CY), here, F32)
        low = link_above * inv_above
        inv = 1.0 / (4.0 + here + link_above - link_above * low)
        lco[k] = low
        cco[k] = inv
        return here, inv

    blocked(LV, factor, (zeros, zeros))
    lco[LV] = zeros

    def shift_sums(k, carry):
        v = sh[k]
        return carry[0] + v, carry[1] + v * v

    sh_sum, sh_sq = blocked(LV, shift_sums, (zeros, zeros))
    edge_w = row8 == 0
    edge_e = row8 == PX - 1
    edge_s = lane == 0
    edge_n = lane == CY - 1

    def edges(v):
        return [jnp.where(m, v, 0.0) for m in (edge_w, edge_e, edge_s, edge_n)]

    shift_row = pack_row([sh_sum, sh_sq] + edges(sh_sum))

    pl.semaphore_wait(barrier, NT - 1 + (NG - 1) * nzh)

    gather_start(0, shift_row)
    a2a_start(hs, hr, 0)
    hr[pl.ds(t, 1), :] = hs[pl.ds(t, 1), :]
    gather_middle(0)

    mass, m_ss, m_sw, m_se, m_sso, m_sn = gather_end(0, 6)
    grow = iota((GP, NT), 0)
    gcol = iota((GP, NT), 1)
    live_s = ((grow > 0) & (grow < NG)).astype(F32)
    live_n = (grow < NG - 1).astype(F32)
    diagonal = mass + 2.0 * LV * CY + LV * PX * (live_s + live_n)
    couple = float(LV * CY)
    b_co = []
    a_co = []
    for j in range(NG):
        entry = jnp.where(grow == j, diagonal, 0.0)
        near = (grow == j - 1) | (grow == j + 1)
        entry = jnp.where(near & (grow < NG), -float(LV * PX), entry)
        b_co.append(entry)
        a_co.append(jnp.where(grow == j, -couple, 0.0))

    def reduce_step(step, carry):
        hop, a_, b_, c_ = carry
        back = NT - hop
        binv = inverse4(b_)
        alpha = matmul4(a_, [roll(v, hop, 1) for v in binv])
        gamma = matmul4(c_, [roll(v, back, 1) for v in binv])
        alpha = [-v for v in alpha]
        gamma = [-v for v in gamma]
        a_m = [roll(v, hop, 1) for v in a_]
        c_m = [roll(v, hop, 1) for v in c_]
        a_p = [roll(v, back, 1) for v in a_]
        c_p = [roll(v, back, 1) for v in c_]
        ac = matmul4(alpha, c_m)
        ga = matmul4(gamma, a_p)
        b_ = [b_[j] + ac[j] + ga[j] for j in range(NG)]
        a_ = matmul4(alpha, a_m)
        c_ = matmul4(gamma, c_p)
        for j in range(NG):
            alpha_co[step, j] = alpha[j]
            gamma_co[step, j] = gamma[j]
        return hop * 2, tuple(a_), tuple(b_), tuple(c_)

    steps = int(math.log2(NT))
    _, a_f, b_f, c_f = lax.fori_loop(
        0, steps, reduce_step, (jnp.int32(1), tuple(a_co), tuple(b_co), tuple(a_co))
    )
    last = inverse4([a_f[j] + b_f[j] + c_f[j] for j in range(NG)])
    for j in range(NG):
        last_co[j] = last[j]

    def coarse_solve(rhs):
        for step in range(steps):
            hop = 1 << step
            low = roll(rhs, hop, 1)
            high = roll(rhs, NT - hop, 1)
            rhs = (
                rhs
                + matvec4([alpha_co[step, j] for j in range(NG)], low)
                + matvec4([gamma_co[step, j] for j in range(NG)], high)
            )
        return matvec4([last_co[j] for j in range(NG)], rhs)

    def differences(e):
        return (
            e - roll(e, 1, 1),
            e - roll(e, NT - 1, 1),
            live_s * (e - roll(e, 1, 0)),
            live_n * (e - roll(e, GP - 1, 0)),
        )

    mine = (grow == g) & (gcol == t)

    def own(v):
        return total(jnp.where(mine, v, 0.0))

    def rim_of(w):
        west, east, south, north = (own(v) for v in w)
        return (
            jnp.where(edge_w, west, 0.0)
            + jnp.where(edge_e, east, 0.0)
            + jnp.where(edge_s, south, 0.0)
            + jnp.where(edge_n, north, 0.0)
        )

    long_rim = float(LV * CY)
    short_rim = float(LV * PX)
    corner = float(LV)
    m_shift = (m_sw, m_se, m_sso, m_sn)

    def own_square(e, w):
        cross = (w[0] + w[1]) * (w[2] + w[3])
        value = e * e * m_ss + long_rim * (w[0] * w[0] + w[1] * w[1])
        value = value + short_rim * (w[2] * w[2] + w[3] * w[3]) + 2.0 * corner * cross
        for i in range(4):
            value = value + 2.0 * e * w[i] * m_shift[i]
        return value

    def against(e, w, with_shift, with_edges):
        value = e * with_shift
        for i in range(4):
            value = value + w[i] * with_edges[i]
        return value

    def column_solve(source, dst):
        def forward(k, above):
            value = source(k) + lco[k] * above
            dst[k] = value
            return value

        blocked(LV, forward, zeros)

        def backward(k, carry):
            below, to_south, to_north = carry
            value = cco[k] * dst[k] + lco[k + 1] * below
            dst[k] = value
            to_south = jnp.where(lane == k, roll(value, k, 1), to_south)
            to_north = jnp.where(lane == k, roll(value, lax.rem(k + 1, CY), 1), to_north)
            return value, to_south, to_north

        return blocked(LV, backward, (zeros, zeros, zeros), reverse=True)

    def halo_copies(n):
        left = (lax.rem(t + NT - 1, NT), g)
        right = (lax.rem(t + 1, NT), g)
        below = (t, lax.rem(g + NG - 1, NG))
        above = (t, lax.rem(g + 1, NG))
        table = (
            (west_send, east_recv, left),
            (east_send, west_recv, right),
            (south_send, north_recv, below),
            (north_send, south_recv, above),
        )
        return [
            pltpu.make_async_remote_copy(
                src_ref=src.at[n],
                dst_ref=dst.at[n],
                send_sem=halo_send_sem.at[n, i],
                recv_sem=halo_recv_sem.at[n, i],
                device_id=device,
                device_id_type=MESH,
            )
            for i, (src, dst, device) in enumerate(table)
        ]

    inner_s = edge_s & (g > 0)
    outer_s = edge_s & (g == 0)
    inner_n = edge_n & (g < NG - 1)
    outer_n = edge_n & (g == NG - 1)

    def halo_start(n, field, rims):
        west_send[n] = field[0:LV, 0, :]
        east_send[n] = field[0:LV, PX - 1, :]
        south_send[n] = rims[1]
        north_send[n] = rims[2]
        copies = halo_copies(n)
        for copy in copies:
            copy.start()
        return copies

    def image_level(n, field, k, south_in, north_in):
        v = field[k]
        west = jnp.where(edge_w, west_recv[n, pl.ds(k, 1), :], roll(v, 1, 0))
        east = jnp.where(edge_e, east_recv[n, pl.ds(k, 1), :], roll(v, PX - 1, 0))
        south = jnp.where(inner_s, roll(south_in, lax.rem(CY - k, CY), 1), roll(v, 1, 1))
        south = jnp.where(outer_s, v, south)
        north = jnp.where(inner_n, roll(north_in, CY - 1 - k, 1), roll(v, CY - 1, 1))
        north = jnp.where(outer_n, v, north)
        return res[k] - ((west + east) + (south + north)) + sh[k] * v

    a2a_wait(0)
    for ch in range(NCH):
        top = min(LV, (ch + 1) * 16)
        block = hr[:, ch * 128 : (ch + 1) * 128].T.reshape(16, PX, CY)
        res[ch * 16 : top] = fv[ch * 16 : top] + block[: top - ch * 16]

    rims = column_solve(lambda k: res[k], smooth0)
    halos = halo_start(0, smooth0, rims)
    for copy in halos:
        copy.wait_recv()
    south_in = south_recv[0]
    north_in = north_recv[0]

    def moments0(k, carry):
        r_sum, q_sum, rq, rs, qq, qs = carry
        q = image_level(0, smooth0, k, south_in, north_in)
        image[k] = q
        r = res[k]
        s = sh[k]
        return r_sum + r, q_sum + q, rq + r * q, rs + r * s, qq + q * q, qs + q * s

    r_sum, q_sum, rq, rs, qq, qs = blocked(LV, moments0, (zeros,) * 6)
    gather_start(1, pack_row([r_sum - q_sum, rq, rs, qq, qs] + edges(r_sum) + edges(q_sum)))
    gather_middle(1)
    got = gather_end(1, 13)
    e0 = coarse_solve(got[0])
    w0 = differences(e0)
    m_rq, m_rs, m_qq, m_qs = got[1:5]
    m_re = got[5:9]
    m_qe = got[9:13]
    projection = total(m_rq + against(e0, w0, m_rs, m_re))
    norm0 = total(m_qq + 2.0 * against(e0, w0, m_qs, m_qe) + own_square(e0, w0))
    step0 = projection / norm0
    left_over = projection - step0 * norm0
    i_s = m_qs + against(e0, w0, m_ss, m_shift)
    i_e = (
        m_qe[0] + e0 * m_sw + long_rim * w0[0] + corner * (w0[2] + w0[3]),
        m_qe[1] + e0 * m_se + long_rim * w0[1] + corner * (w0[2] + w0[3]),
        m_qe[2] + e0 * m_sso + short_rim * w0[2] + corner * (w0[0] + w0[1]),
        m_qe[3] + e0 * m_sn + short_rim * w0[3] + corner * (w0[0] + w0[1]),
    )
    e0_own = own(e0)
    rim0 = rim_of(w0)

    def next_residual(k):
        q = image[k] + sh[k] * e0_own + rim0
        image[k] = q
        r = res[k] - step0 * q
        res[k] = r
        return r

    rims = column_solve(next_residual, smooth1)
    halos1 = halo_start(1, smooth1, rims)
    for copy in halos1:
        copy.wait_recv()
    south_in1 = south_recv[1]
    north_in1 = north_recv[1]

    def moments1(k, carry):
        r_sum, q_sum, rq, rs, qq, qs, iq = carry
        q = image_level(1, smooth1, k, south_in1, north_in1)
        r = res[k]
        s = sh[k]
        return (
            r_sum + r,
            q_sum + q,
            rq + r * q,
            rs + r * s,
            qq + q * q,
            qs + q * s,
            iq + image[k] * q,
        )

    r_sum, q_sum, rq, rs, qq, qs, iq = blocked(LV, moments1, (zeros,) * 7)
    gather_start(2, pack_row([r_sum - q_sum, rq, rs, qq, qs] + edges(r_sum) + edges(q_sum) + [iq]))
    gather_middle(2)
    got = gather_end(2, 14)
    e1 = coarse_solve(got[0])
    w1 = differences(e1)
    m_rq, m_rs, m_qq, m_qs = got[1:5]
    m_re = got[5:9]
    m_qe = got[9:13]
    crossing = total(got[13] + against(e1, w1, i_s, i_e))
    projection1 = total(m_rq + against(e1, w1, m_rs, m_re))
    square1 = total(m_qq + 2.0 * against(e1, w1, m_qs, m_qe) + own_square(e1, w1))
    weight = crossing / norm0
    norm1 = square1 - weight * crossing
    step1 = (projection1 - weight * left_over) / norm1
    scale0 = step0 - step1 * weight
    constant = scale0 * e0_own + step1 * own(e1)

    def finish(k, _):
        out_field[k] = scale0 * smooth0[k] + step1 * smooth1[k] + constant
        return 0

    blocked(LV, finish, 0)
    for ch in range(NCH):
        top = min(LV, (ch + 1) * 16)
        block = out_field[ch * 16 : top]
        if top < (ch + 1) * 16:
            block = jnp.concatenate([block, jnp.zeros(((ch + 1) * 16 - top, PX, CY), F32)], axis=0)
        xs[:, ch * 128 : (ch + 1) * 128] = block.reshape(16 * PX, CY).T
    a2a_start(xs, xr, 1)
    xr[pl.ds(t, 1), :] = xs[pl.ds(t, 1), :]
    a2a_wait(1)
    for ch in range(NCH):
        top = min(LV, (ch + 1) * 16)
        block = xr[:, ch * 128 : (ch + 1) * 128].T.reshape(16, PX, CY)
        out_rad[ch * 16 : top] = block[: top - ch * 16]

    a2a_drain(0)
    a2a_drain(1)
    for copy in halos + halos1:
        copy.wait_send()
    for which in range(3):
        gather_drain(which)


def per_device(fv, sh, link, kel, longwave, shortwave):
    vmem = pl.BlockSpec(memory_space=pltpu.VMEM)
    smem = pl.BlockSpec(memory_space=pltpu.SMEM)
    field = jax.ShapeDtypeStruct((LV, PX, CY), F32)
    np_ = DIMS[0] * DIMS[2] * DIMS[3]
    steps = int(math.log2(NT))
    padded = pltpu.VMEM((LP, PX, CY), F32)
    lines = pltpu.VMEM((NT, LP * PX), F32)
    rims = pltpu.VMEM((2, LV, CY), F32)
    corners = pltpu.VMEM((2, PX, CY), F32)
    dma = pltpu.SemaphoreType.DMA
    return pl.pallas_call(
        kernel,
        out_shape=(field, field),
        in_specs=[vmem, vmem, vmem, smem, smem, smem],
        out_specs=(vmem, vmem),
        scratch_shapes=[padded] * 8
        + [lines] * 4
        + [rims, rims, corners, corners, rims, rims, corners, corners]
        + [
            pltpu.VMEM((3, DIMS[1] * NG, 128), F32),
            pltpu.VMEM((3, np_, NM // 8, 128), F32),
            pltpu.VMEM((steps, NG, GP, NT), F32),
            pltpu.VMEM((steps, NG, GP, NT), F32),
            pltpu.VMEM((NG, GP, NT), F32),
            pltpu.VMEM((NT - 1, 1, LP * PX), F32),
            pltpu.VMEM((DIMS[1] * NG, 1, 128), F32),
            dma((2,)),
            dma((2,)),
            dma((2, 4)),
            dma((2, 4)),
            dma((3,)),
            dma((3,)),
            dma((3,)),
            dma((3,)),
        ],
        compiler_params=pltpu.CompilerParams(
            collective_id=0, has_side_effects=True, vmem_limit_bytes=32 << 20
        ),
        name="step",
    )(fv, sh, kel, link, longwave, shortwave)


def solution(mesh):
    spread = P(None, "tile", "grp")
    columns = P(None, None, ("tile", "grp"))
    return jax.shard_map(
        per_device,
        mesh=mesh,
        in_specs=(spread, spread, P(), columns, P(), P()),
        out_specs=(spread, columns),
        check_vma=False,
    )
```

```python
import math

import jax
import jax.numpy as jnp
from jax import lax
from jax.experimental import pallas as pl
from jax.experimental.pallas import tpu as pltpu
from jax.sharding import PartitionSpec as P

LV = 70
PX = 8
CY = 128
NG = 4
DIMS = (4, 4, 4, 2)
NT = 128
LP = 80
NCH = LP // 16
UNROLL = 10
NM = 16
GP = 8
F32 = jnp.float32
MESH = pl.DeviceIdType.MESH


def iota(shape, dim):
    return lax.broadcasted_iota(jnp.int32, shape, dim)


def roll(value, shift, axis):
    return pltpu.roll(value, shift, axis)


def blocked(levels, body, init, reverse=False):
    def trip(b, carry):
        for j in range(UNROLL):
            k = b * UNROLL + j
            carry = body(levels - 1 - k if reverse else k, carry)
        return carry

    return lax.fori_loop(0, levels // UNROLL, trip, init)


def total(value):
    return jnp.sum(jnp.sum(value, axis=0, keepdims=True), axis=1, keepdims=True)


def matmul4(left, right):
    out = []
    for j in range(NG):
        term = left[0] * right[j][0:1, :]
        for l in range(1, NG):
            term = term + left[l] * right[j][l : l + 1, :]
        out.append(term)
    return out


def inverse4(columns):
    columns = list(columns)
    row = iota((GP, NT), 0)
    for k in range(NG):
        pivot = 1.0 / columns[k][k : k + 1, :]
        for j in range(NG):
            if j != k:
                scaled = columns[j][k : k + 1, :] * pivot
                columns[j] = jnp.where(row == k, scaled, columns[j] - columns[k] * scaled)
        columns[k] = jnp.where(row == k, pivot, -columns[k] * pivot)
    return columns


def matvec4(columns, vector):
    out = columns[0] * vector[0:1, :]
    for l in range(1, NG):
        out = out + columns[l] * vector[l : l + 1, :]
    return out


def kernel(
    fv_hbm,
    sh_hbm,
    kel_hbm,
    link_hbm,
    longwave_hbm,
    shortwave_hbm,
    out_field,
    out_rad,
    fv,
    sh,
    kel,
    link,
    longwave,
    shortwave,
    down,
    upw,
    lco,
    cco,
    res,
    smooth0,
    smooth1,
    image,
    shift_solve,
    image_solve,
    hs,
    hr,
    fs,
    fr,
    xs,
    xr,
    west_send,
    east_send,
    south_send,
    north_send,
    west_recv,
    east_recv,
    south_recv,
    north_recv,
    zbuf,
    pbuf,
    alpha_co,
    gamma_co,
    last_co,
    line_count,
    row_count,
    ghost_west,
    ghost_east,
    in_sem,
    a2a_send_sem,
    a2a_recv_sem,
    halo_send_sem,
    halo_recv_sem,
    z_send_sem,
    z_recv_sem,
    p_send_sem,
    p_recv_sem,
):
    ny, nzh, nx, nc = DIMS
    nz = nzh * NG
    np_ = ny * nx * nc
    t = lax.axis_index("tile")
    g = lax.axis_index("grp")
    c = lax.rem(t, nc)
    x = lax.rem(lax.div(t, nc), nx)
    zh = lax.rem(lax.div(t, nc * nx), nzh)
    y = lax.div(t, nc * nx * nzh)
    z = zh * NG + g
    p = (y * nx + x) * nc + c

    def tile_of(y_, zh_, x_, c_):
        return ((y_ * nzh + zh_) * nx + x_) * nc + c_

    z_part = [lax.rem(zh + dz, nzh) * (nx * nc) for dz in range(nzh)]
    z_order = sorted(range(nzh), key=lambda dz: -min(dz, nzh - dz))

    def plane_base(r):
        dc = lax.rem(r, nc)
        dx = lax.rem(lax.div(r, nc), nx)
        dy = lax.div(r, nc * nx)
        low = lax.rem(x + dx, nx) * nc + lax.rem(c + dc, nc)
        return lax.rem(y + dy, ny) * (nzh * nx * nc) + low

    def each_tile(low, high, act):
        if low == 0:
            base = plane_base(0)
            for dz in z_order[:-1]:
                act(base + z_part[dz])

        def some(r, _):
            base = plane_base(r)
            for dz in z_order:
                act(base + z_part[dz])
            return 0

        lax.fori_loop(max(low, 1), high, some, 0)

    plane_here = plane_base(0)

    def each_z(first, act):
        if first == 0:
            for dz in z_order[:-1]:
                act(plane_here + z_part[dz], g)

        def some(dg, _):
            g2 = lax.rem(g + dg, NG)
            for dz in z_order:
                act(plane_here + z_part[dz], g2)
            return 0

        lax.fori_loop(1, NG, some, 0)

    barrier = pltpu.get_barrier_semaphore()

    def greet(tile, grp):
        pl.semaphore_signal(barrier, inc=1, device_id=(tile, grp), device_id_type=MESH)

    each_z(1, greet)
    each_tile(0, np_, lambda tile: greet(tile, g))
    pairs = (
        (kel_hbm, kel),
        (longwave_hbm, longwave),
        (shortwave_hbm, shortwave),
        (link_hbm, link),
        (sh_hbm, sh),
        (fv_hbm, fv.at[pl.ds(0, LV)]),
    )
    loads = [pltpu.make_async_copy(src, dst, in_sem.at[i]) for i, (src, dst) in enumerate(pairs)]
    for load in loads:
        load.start()
    for load in loads:
        load.wait()

    def wait_lines(sem):
        pltpu.make_async_copy(line_count, line_count, sem).wait()

    def wait_rows(sem):
        rows = row_count.at[pl.ds(0, nz - 1)]
        pltpu.make_async_copy(rows, rows, sem).wait()

    def a2a_start(src, dst, which, low, high):
        def send(peer):
            pltpu.make_async_remote_copy(
                src_ref=src.at[pl.ds(peer, 1), :],
                dst_ref=dst.at[pl.ds(t, 1), :],
                send_sem=a2a_send_sem.at[which],
                recv_sem=a2a_recv_sem.at[which],
                device_id=(peer, g),
                device_id_type=MESH,
            ).start()

        each_tile(low, high, send)

    def a2a_wait(which):
        wait_lines(a2a_recv_sem.at[which])

    def a2a_drain(which):
        wait_lines(a2a_send_sem.at[which])

    lane = iota((PX, CY), 1)
    row8 = iota((PX, CY), 0)

    def pack_row(values):
        rows = [jnp.sum(v, axis=0, keepdims=True) for v in values]
        rows = rows + [jnp.zeros((1, CY), F32)] * (NM - len(rows))
        sums = jnp.sum(jnp.concatenate(rows, axis=0), axis=1, keepdims=True)
        diag = iota((NM, 128), 0) == iota((NM, 128), 1)
        return jnp.sum(jnp.where(diag, sums, 0.0), axis=0, keepdims=True)

    def gather_start(which, row):
        buf = zbuf.at[which]
        buf[pl.ds(z, 1), :] = row

        def send(tile, grp):
            pltpu.make_async_remote_copy(
                src_ref=buf.at[pl.ds(z, 1), :],
                dst_ref=buf.at[pl.ds(z, 1), :],
                send_sem=z_send_sem.at[which],
                recv_sem=z_recv_sem.at[which],
                device_id=(tile, grp),
                device_id_type=MESH,
            ).start()

        each_z(0, send)

    def gather_middle(which):
        buf = zbuf.at[which]
        wait_rows(z_recv_sem.at[which])
        value = buf[...]
        ln = iota((nz, 128), 1)
        mine = lax.rem(ln, nz) == iota((nz, 128), 0)
        packed = []
        for r in range(NM // 8):
            spread = jnp.take_along_axis(value, lax.rem(r * 8 + lax.div(ln, nz), 128), axis=1)
            packed.append(jnp.sum(jnp.where(mine, spread, 0.0), axis=0, keepdims=True))
        pbuf[which, pl.ds(p, 1)] = jnp.concatenate(packed, axis=0)[None]
        dst = pbuf.at[which]

        def send(r, _):
            pltpu.make_async_remote_copy(
                src_ref=dst.at[pl.ds(p, 1)],
                dst_ref=dst.at[pl.ds(p, 1)],
                send_sem=p_send_sem.at[which],
                recv_sem=p_recv_sem.at[which],
                device_id=(plane_base(r) + z_part[0], g),
                device_id_type=MESH,
            ).start()
            return 0

        lax.fori_loop(1, np_, send, 0)

    def gather_end(which, count):
        rows = pbuf.at[which, pl.ds(0, np_ - 1)]
        pltpu.make_async_copy(rows, rows, p_recv_sem.at[which]).wait()
        parts = [pbuf[which, :, r, :] for r in range(NM // 8)]
        parts.append(jnp.zeros((128 - np_ * (NM // 8), 128), F32))
        flat = jnp.concatenate(parts, axis=0).T
        ln = iota((128, 128), 1)
        rw = iota((128, 128), 0)
        t_p = (lax.rem(lax.div(ln, nc * nx * nzh), ny) * nx * nc) + lax.rem(ln, nx * nc)
        t_zh = lax.rem(lax.div(ln, nc * nx), nzh)
        keep = lax.div(lax.rem(rw, nz), NG) == t_zh
        found = []
        for r in range(NM // 8):
            if len(found) >= count:
                break
            got = jnp.take_along_axis(flat, t_p + r * np_, axis=1)
            got = jnp.where(keep, got, 0.0)
            for m in range(8):
                if len(found) >= count:
                    break
                block = got[m * nz : (m + 1) * nz, :NT]
                acc = block[0:NG]
                for b in range(1, nzh):
                    acc = acc + block[b * NG : (b + 1) * NG]
                found.append(jnp.concatenate([acc, jnp.zeros((GP - NG, NT), F32)], axis=0))
        return found

    def gather_drain(which):
        wait_rows(z_send_sem.at[which])
        rows = pbuf.at[which, pl.ds(0, np_ - 1)]
        pltpu.make_async_copy(rows, rows, p_send_sem.at[which]).wait()

    zeros = jnp.zeros((PX, CY), F32)
    latitude = ((g * CY + t).astype(F32) + 0.5) / float(CY * NG) - 0.5
    mu10 = 10.0 * jnp.cos(jnp.full((PX, CY), latitude * (math.pi / 2) - 0.4, F32))

    def emission(k):
        square = kel[k] * kel[k]
        return square * square

    def both_passes(k, carry):
        flux_down, flux_up, sun, acc = carry
        em = emission(k)
        trans = jnp.exp(jnp.full((PX, CY), -longwave[k], F32))
        absorbed = 1.0 - trans
        sun_trans = jnp.exp(jnp.full((PX, CY), -shortwave[k], F32))
        raw = absorbed * (flux_down - 2.0 * em) + mu10 * (sun * (1.0 - sun_trans))
        down[k] = raw
        flux_down = trans * flux_down + absorbed * em
        sun = sun * sun_trans
        k2 = LV - 1 - k
        em2 = emission(k2)
        trans2 = jnp.exp(jnp.full((PX, CY), -longwave[k2], F32))
        absorbed2 = 1.0 - trans2
        raw2 = absorbed2 * flux_up
        upw[k2] = raw2
        flux_up = trans2 * flux_up + absorbed2 * em2
        return flux_down, flux_up, sun, acc + (raw + raw2)

    carry = blocked(LV, both_passes, (zeros, emission(LV - 1), jnp.ones((PX, CY), F32), zeros))
    mean = carry[3] * (1.0 / LV)
    for k in range(LV, LP):
        fv[k] = zeros
        smooth1[k] = zeros
        down[k] = zeros
        upw[k] = zeros
        res[k] = zeros
    for ch in range(NCH):
        lv = slice(ch * 16, (ch + 1) * 16)
        heat = down[lv] + upw[lv] - mean[None]
        down[lv] = heat
        hs[:, ch * 128 : (ch + 1) * 128] = heat.reshape(16 * PX, CY).T

    def lines_of(field, dst):
        for ch in range(NCH):
            dst[:, ch * 128 : (ch + 1) * 128] = (
                field[ch * 16 : (ch + 1) * 16].reshape(16 * PX, CY).T
            )

    def columns_of(src, ch):
        top = min(LV, (ch + 1) * 16)
        block = src[:, ch * 128 : (ch + 1) * 128].T.reshape(16, PX, CY)
        return slice(ch * 16, top), block[: top - ch * 16]

    lines_of(fv, fs)

    def factor(k, carry):
        link_above, inv_above = carry
        here = jnp.where(k < LV - 1, link[jnp.minimum(k, LV - 2)], 0.0)
        here = jnp.full((PX, CY), here, F32)
        low = link_above * inv_above
        inv = 1.0 / (4.0 + here + link_above - link_above * low)
        lco[k] = low
        cco[k] = inv
        return here, inv

    blocked(LV, factor, (zeros, zeros))
    lco[LV] = zeros

    def shift_sums(k, carry):
        v = sh[k]
        return carry[0] + v, carry[1] + v * v

    sh_sum, sh_sq = blocked(LV, shift_sums, (zeros, zeros))
    edge_w = row8 == 0
    edge_e = row8 == PX - 1
    edge_s = lane == 0
    edge_n = lane == CY - 1

    def edges(v):
        return [jnp.where(m, v, 0.0) for m in (edge_w, edge_e, edge_s, edge_n)]

    shift_row = pack_row([sh_sum, sh_sq] + edges(sh_sum))

    def column_solve(source, dst):
        def forward(k, above):
            value = source(k) + lco[k] * above
            dst[k] = value
            return value

        blocked(LV, forward, zeros)

        def backward(k, carry):
            below, to_south, to_north = carry
            value = cco[k] * dst[k] + lco[k + 1] * below
            dst[k] = value
            to_south = jnp.where(lane == k, roll(value, k, 1), to_south)
            to_north = jnp.where(lane == k, roll(value, lax.rem(k + 1, CY), 1), to_north)
            return value, to_south, to_north

        return blocked(LV, backward, (zeros, zeros, zeros), reverse=True)

    def halo_copies(n):
        left = (lax.rem(t + NT - 1, NT), g)
        right = (lax.rem(t + 1, NT), g)
        below = (t, lax.rem(g + NG - 1, NG))
        above = (t, lax.rem(g + 1, NG))
        table = (
            (west_send, east_recv, left),
            (east_send, west_recv, right),
            (south_send, north_recv, below),
            (north_send, south_recv, above),
        )
        return [
            pltpu.make_async_remote_copy(
                src_ref=src.at[n],
                dst_ref=dst.at[n],
                send_sem=halo_send_sem.at[n, i],
                recv_sem=halo_recv_sem.at[n, i],
                device_id=device,
                device_id_type=MESH,
            )
            for i, (src, dst, device) in enumerate(table)
        ]

    def halo_fill(n, field, rims):
        west_send[n] = field[0:LV, 0, :]
        east_send[n] = field[0:LV, PX - 1, :]
        south_send[n] = rims[1]
        north_send[n] = rims[2]

    def halo_start(n):
        copies = halo_copies(n)
        for copy in copies:
            copy.start()
        return copies

    def plain_solve(field, dst):
        def forward(k, above):
            value = field[k] + lco[k] * above
            dst[k] = value
            return value

        blocked(LV, forward, zeros)

        def backward(k, below):
            value = cco[k] * dst[k] + lco[k + 1] * below
            dst[k] = value
            return value

        blocked(LV, backward, zeros, reverse=True)

    shift_rims = column_solve(lambda k: sh[k], shift_solve)
    halo_fill(2, shift_solve, shift_rims)

    pl.semaphore_wait(barrier, NT - 1 + (NG - 1) * nzh)

    gather_start(0, shift_row)
    a2a_start(hs, hr, 0, 0, np_)
    hr[pl.ds(t, 1), :] = hs[pl.ds(t, 1), :]
    fr[pl.ds(t, 1), :] = fs[pl.ds(t, 1), :]
    halos2 = halo_start(2)
    gather_middle(0)

    mass, m_ss, m_sw, m_se, m_sso, m_sn = gather_end(0, 6)
    grow = iota((GP, NT), 0)
    gcol = iota((GP, NT), 1)
    live_s = ((grow > 0) & (grow < NG)).astype(F32)
    live_n = (grow < NG - 1).astype(F32)
    diagonal = mass + 2.0 * LV * CY + LV * PX * (live_s + live_n)
    couple = float(LV * CY)
    b_co = []
    a_co = []
    for j in range(NG):
        entry = jnp.where(grow == j, diagonal, 0.0)
        near = (grow == j - 1) | (grow == j + 1)
        entry = jnp.where(near & (grow < NG), -float(LV * PX), entry)
        b_co.append(entry)
        a_co.append(jnp.where(grow == j, -couple, 0.0))

    def reduce_step(step, carry):
        hop, a_, b_, c_ = carry
        back = NT - hop
        binv = inverse4(b_)
        alpha = matmul4(a_, [roll(v, hop, 1) for v in binv])
        gamma = matmul4(c_, [roll(v, back, 1) for v in binv])
        alpha = [-v for v in alpha]
        gamma = [-v for v in gamma]
        a_m = [roll(v, hop, 1) for v in a_]
        c_m = [roll(v, hop, 1) for v in c_]
        a_p = [roll(v, back, 1) for v in a_]
        c_p = [roll(v, back, 1) for v in c_]
        ac = matmul4(alpha, c_m)
        ga = matmul4(gamma, a_p)
        b_ = [b_[j] + ac[j] + ga[j] for j in range(NG)]
        a_ = matmul4(alpha, a_m)
        c_ = matmul4(gamma, c_p)
        for j in range(NG):
            alpha_co[step, j] = alpha[j]
            gamma_co[step, j] = gamma[j]
        return hop * 2, tuple(a_), tuple(b_), tuple(c_)

    steps = int(math.log2(NT))
    _, a_f, b_f, c_f = lax.fori_loop(
        0, steps, reduce_step, (jnp.int32(1), tuple(a_co), tuple(b_co), tuple(a_co))
    )
    last = inverse4([a_f[j] + b_f[j] + c_f[j] for j in range(NG)])
    for j in range(NG):
        last_co[j] = last[j]

    def coarse_solve(rhs):
        for step in range(steps):
            hop = 1 << step
            low = roll(rhs, hop, 1)
            high = roll(rhs, NT - hop, 1)
            rhs = (
                rhs
                + matvec4([alpha_co[step, j] for j in range(NG)], low)
                + matvec4([gamma_co[step, j] for j in range(NG)], high)
            )
        return matvec4([last_co[j] for j in range(NG)], rhs)

    def differences(e):
        return (
            e - roll(e, 1, 1),
            e - roll(e, NT - 1, 1),
            live_s * (e - roll(e, 1, 0)),
            live_n * (e - roll(e, GP - 1, 0)),
        )

    mine = (grow == g) & (gcol == t)

    def own(v):
        return total(jnp.where(mine, v, 0.0))

    def rim_of(west, east, south, north):
        return (
            jnp.where(edge_w, west, 0.0)
            + jnp.where(edge_e, east, 0.0)
            + jnp.where(edge_s, south, 0.0)
            + jnp.where(edge_n, north, 0.0)
        )

    long_rim = float(LV * CY)
    short_rim = float(LV * PX)
    corner = float(LV)
    m_shift = (m_sw, m_se, m_sso, m_sn)

    def own_square(e, w):
        cross = (w[0] + w[1]) * (w[2] + w[3])
        value = e * e * m_ss + long_rim * (w[0] * w[0] + w[1] * w[1])
        value = value + short_rim * (w[2] * w[2] + w[3] * w[3]) + 2.0 * corner * cross
        for i in range(4):
            value = value + 2.0 * e * w[i] * m_shift[i]
        return value

    def against(e, w, with_shift, with_edges):
        value = e * with_shift
        for i in range(4):
            value = value + w[i] * with_edges[i]
        return value

    inner_s = edge_s & (g > 0)
    outer_s = edge_s & (g == 0)
    inner_n = edge_n & (g < NG - 1)
    outer_n = edge_n & (g == NG - 1)

    def image_level(v, r, k, west_in, east_in, south_in, north_in):
        west = jnp.where(edge_w, west_in[pl.ds(k, 1), :], roll(v, 1, 0))
        east = jnp.where(edge_e, east_in[pl.ds(k, 1), :], roll(v, PX - 1, 0))
        south = jnp.where(inner_s, roll(south_in, lax.rem(CY - k, CY), 1), roll(v, 1, 1))
        south = jnp.where(outer_s, v, south)
        north = jnp.where(inner_n, roll(north_in, CY - 1 - k, 1), roll(v, CY - 1, 1))
        north = jnp.where(outer_n, v, north)
        return r - ((west + east) + (south + north)) + sh[k] * v

    a2a_wait(0)
    for ch in range(NCH):
        lv, block = columns_of(hr, ch)
        res[lv] = fv[lv] + block

    half = np_ // 2
    rims = column_solve(lambda k: res[k], smooth0)
    halo_fill(0, smooth0, rims)
    halos0 = halo_start(0)
    a2a_start(fs, fr, 1, 0, half)
    for copy in halos0:
        copy.wait_recv()
    south_in = south_recv[0]
    north_in = north_recv[0]

    def moments0(k, carry):
        r_sum, q_sum, rq, rs, qq, qs = carry
        r = res[k]
        q = image_level(
            smooth0[k], r, k, west_recv.at[0], east_recv.at[0], south_in, north_in
        )
        image[k] = q
        s = sh[k]
        return r_sum + r, q_sum + q, rq + r * q, rs + r * s, qq + q * q, qs + q * s

    r_sum, q_sum, rq, rs, qq, qs = blocked(LV, moments0, (zeros,) * 6)
    gather_start(1, pack_row([r_sum - q_sum, rq, rs, qq, qs] + edges(r_sum) + edges(q_sum)))
    image_rims = column_solve(lambda k: image[k], image_solve)
    halo_fill(1, image_solve, image_rims)
    halos1 = halo_start(1)
    a2a_start(fs, fr, 1, half, np_)
    gather_middle(1)
    got = gather_end(1, 13)
    e0 = coarse_solve(got[0])
    w0 = differences(e0)
    m_rq, m_rs, m_qq, m_qs = got[1:5]
    m_re = got[5:9]
    m_qe = got[9:13]
    projection = total(m_rq + against(e0, w0, m_rs, m_re))
    norm0 = total(m_qq + 2.0 * against(e0, w0, m_qs, m_qe) + own_square(e0, w0))
    step0 = projection / norm0
    left_over = projection - step0 * norm0
    i_s = m_qs + against(e0, w0, m_ss, m_shift)
    i_e = (
        m_qe[0] + e0 * m_sw + long_rim * w0[0] + corner * (w0[2] + w0[3]),
        m_qe[1] + e0 * m_se + long_rim * w0[1] + corner * (w0[2] + w0[3]),
        m_qe[2] + e0 * m_sso + short_rim * w0[2] + corner * (w0[0] + w0[1]),
        m_qe[3] + e0 * m_sn + short_rim * w0[3] + corner * (w0[0] + w0[1]),
    )
    at_west = (grow == g) & (gcol == lax.rem(t + NT - 1, NT))
    at_east = (grow == g) & (gcol == lax.rem(t + 1, NT))
    at_south = (grow == g - 1) & (gcol == t)
    at_north = (grow == g + 1) & (gcol == t)
    wanted = [(m, e0) for m in (mine, at_west, at_east, at_south, at_north)]
    wanted = wanted + [(mine, v) for v in w0]
    wanted = wanted + [(at_west, w0[i]) for i in (1, 2, 3)]
    wanted = wanted + [(at_east, w0[i]) for i in (0, 2, 3)]
    wanted = wanted + [(at_south, w0[i]) for i in (3, 0, 1)]
    wanted = wanted + [(at_north, w0[i]) for i in (2, 0, 1)]
    found = [jnp.sum(jnp.where(m, v, 0.0), axis=0, keepdims=True) for m, v in wanted]
    found = found + [jnp.zeros((1, NT), F32)] * (24 - len(found))
    found = jnp.sum(jnp.concatenate(found, axis=0), axis=1, keepdims=True)
    found = [found[i : i + 1] for i in range(21)]
    e0_own, e_west, e_east, e_south, e_north = found[0:5]
    rim0 = rim_of(*found[5:9])
    lane1 = iota((1, CY), 1)
    row1 = iota((PX, 1), 0)

    def rim_row(f):
        return f[0] + jnp.where(lane1 == 0, f[1], 0.0) + jnp.where(lane1 == CY - 1, f[2], 0.0)

    def rim_col(f):
        return f[0] + jnp.where(row1 == 0, f[1], 0.0) + jnp.where(row1 == PX - 1, f[2], 0.0)

    for copy in halos2 + halos1:
        copy.wait_recv()

    def ghost(recv, e, rim):
        return recv[0] - step0 * (recv[1] + e * recv[2] + 0.25 * rim)

    ghost_west[...] = ghost(west_recv, e_west, rim_row(found[9:12]))
    ghost_east[...] = ghost(east_recv, e_east, rim_row(found[12:15]))
    ghost_south = ghost(south_recv, e_south, rim_col(found[15:18]))
    ghost_north = ghost(north_recv, e_north, rim_col(found[18:21]))

    quarter_rim = 0.25 * rim0

    def moments1(k, carry):
        r_sum, q_sum, rq, rs, qq, qs, iq = carry
        s = sh[k]
        q0 = image[k] + s * e0_own + rim0
        r = res[k] - step0 * q0
        v = smooth0[k] - step0 * (image_solve[k] + e0_own * shift_solve[k] + quarter_rim)
        smooth1[k] = v
        q = image_level(v, r, k, ghost_west, ghost_east, ghost_south, ghost_north)
        return (
            r_sum + r,
            q_sum + q,
            rq + r * q,
            rs + r * s,
            qq + q * q,
            qs + q * s,
            iq + q0 * q,
        )

    r_sum, q_sum, rq, rs, qq, qs, iq = blocked(LV, moments1, (zeros,) * 7)
    gather_start(2, pack_row([r_sum - q_sum, rq, rs, qq, qs] + edges(r_sum) + edges(q_sum) + [iq]))
    lines_of(smooth1, xs)
    a2a_start(xs, xr, 2, 0, half)
    xr[pl.ds(t, 1), :] = xs[pl.ds(t, 1), :]

    a2a_wait(1)
    for ch in range(NCH):
        lv, block = columns_of(fr, ch)
        down[lv] = down[lv] + block
    plain_solve(down, upw)

    gather_middle(2)
    a2a_start(xs, xr, 2, half, np_)
    got = gather_end(2, 14)
    e1 = coarse_solve(got[0])
    w1 = differences(e1)
    m_rq, m_rs, m_qq, m_qs = got[1:5]
    m_re = got[5:9]
    m_qe = got[9:13]
    crossing = total(got[13] + against(e1, w1, i_s, i_e))
    projection1 = total(m_rq + against(e1, w1, m_rs, m_re))
    square1 = total(m_qq + 2.0 * against(e1, w1, m_qs, m_qe) + own_square(e1, w1))
    weight = crossing / norm0
    norm1 = square1 - weight * crossing
    step1 = (projection1 - weight * left_over) / norm1
    scale0 = step0 - step1 * weight
    block_part = scale0 * e0 + step1 * e1
    constant = own(block_part)
    by_tile = jnp.sum(jnp.where(grow == g, block_part, 0.0), axis=0, keepdims=True)

    def finish(k, _):
        out_field[k] = scale0 * smooth0[k] + step1 * smooth1[k] + constant
        return 0

    blocked(LV, finish, 0)

    a2a_wait(2)
    for ch in range(NCH):
        lv, block = columns_of(xr, ch)
        out_rad[lv] = scale0 * upw[lv] + step1 * block + by_tile[None]

    for which in range(3):
        a2a_drain(which)
        gather_drain(which)
    for copy in halos0 + halos1 + halos2:
        copy.wait_send()


def per_device(fv, sh, link, kel, longwave, shortwave):
    vmem = pl.BlockSpec(memory_space=pltpu.VMEM)
    hbm = pl.BlockSpec(memory_space=pltpu.HBM)
    field = jax.ShapeDtypeStruct((LV, PX, CY), F32)
    np_ = DIMS[0] * DIMS[2] * DIMS[3]
    steps = int(math.log2(NT))
    padded = pltpu.VMEM((LP, PX, CY), F32)
    whole = pltpu.VMEM((LV, PX, CY), F32)
    lines = pltpu.VMEM((NT, LP * PX), F32)
    rims = pltpu.VMEM((3, LV, CY), F32)
    corners = pltpu.VMEM((3, PX, CY), F32)
    dma = pltpu.SemaphoreType.DMA
    return pl.pallas_call(
        kernel,
        out_shape=(field, field),
        in_specs=[hbm] * 6,
        out_specs=(vmem, vmem),
        scratch_shapes=[padded, whole, whole]
        + [pltpu.SMEM((LV - 1,), F32), pltpu.SMEM((LV,), F32), pltpu.SMEM((LV,), F32)]
        + [padded] * 10
        + [lines] * 6
        + [rims, rims, corners, corners, rims, rims, corners, corners]
        + [
            pltpu.VMEM((3, DIMS[1] * NG, 128), F32),
            pltpu.VMEM((3, np_, NM // 8, 128), F32),
            pltpu.VMEM((steps, NG, GP, NT), F32),
            pltpu.VMEM((steps, NG, GP, NT), F32),
            pltpu.VMEM((NG, GP, NT), F32),
            pltpu.VMEM((NT - 1, 1, LP * PX), F32),
            pltpu.VMEM((DIMS[1] * NG, 1, 128), F32),
            pltpu.VMEM((LV, CY), F32),
            pltpu.VMEM((LV, CY), F32),
            dma((6,)),
            dma((3,)),
            dma((3,)),
            dma((3, 4)),
            dma((3, 4)),
            dma((3,)),
            dma((3,)),
            dma((3,)),
            dma((3,)),
        ],
        compiler_params=pltpu.CompilerParams(
            collective_id=0, has_side_effects=True, vmem_limit_bytes=32 << 20
        ),
        name="step",
    )(fv, sh, kel, link, longwave, shortwave)


def solution(mesh):
    spread = P(None, "tile", "grp")
    columns = P(None, None, ("tile", "grp"))
    return jax.shard_map(
        per_device,
        mesh=mesh,
        in_specs=(spread, spread, P(), columns, P(), P()),
        out_specs=(spread, columns),
        check_vma=False,
    )
```

```python
import math

import jax
import jax.numpy as jnp
from jax import lax
from jax.experimental import pallas as pl
from jax.experimental.pallas import tpu as pltpu
from jax.sharding import PartitionSpec as P

LV = 70
PX = 8
CY = 128
NG = 4
DIMS = (4, 4, 4, 2)
NT = 128
LP = 80
NCH = LP // 16
UNROLL = 10
NM = 16
GP = 8
F32 = jnp.float32
MESH = pl.DeviceIdType.MESH


def iota(shape, dim):
    return lax.broadcasted_iota(jnp.int32, shape, dim)


def roll(value, shift, axis):
    return pltpu.roll(value, shift, axis)


def blocked(levels, body, init, reverse=False):
    def trip(b, carry):
        for j in range(UNROLL):
            k = b * UNROLL + j
            carry = body(levels - 1 - k if reverse else k, carry)
        return carry

    return lax.fori_loop(0, levels // UNROLL, trip, init)


def total(value):
    return jnp.sum(jnp.sum(value, axis=0, keepdims=True), axis=1, keepdims=True)


def matmul4(left, right):
    out = []
    for j in range(NG):
        term = left[0] * right[j][0:1, :]
        for l in range(1, NG):
            term = term + left[l] * right[j][l : l + 1, :]
        out.append(term)
    return out


def inverse4(columns):
    columns = list(columns)
    row = iota((GP, NT), 0)
    for k in range(NG):
        pivot = 1.0 / columns[k][k : k + 1, :]
        for j in range(NG):
            if j != k:
                scaled = columns[j][k : k + 1, :] * pivot
                columns[j] = jnp.where(row == k, scaled, columns[j] - columns[k] * scaled)
        columns[k] = jnp.where(row == k, pivot, -columns[k] * pivot)
    return columns


def matvec4(columns, vector):
    out = columns[0] * vector[0:1, :]
    for l in range(1, NG):
        out = out + columns[l] * vector[l : l + 1, :]
    return out


def kernel(
    fv_hbm,
    sh_hbm,
    kel_hbm,
    link_hbm,
    longwave_hbm,
    shortwave_hbm,
    out_field,
    out_rad,
    fv,
    sh,
    kel,
    link,
    longwave,
    shortwave,
    down,
    upw,
    lco,
    cco,
    res,
    smooth0,
    smooth1,
    image,
    shift_solve,
    image_solve,
    hs,
    hr,
    fs,
    fr,
    xs,
    xr,
    west_send,
    east_send,
    south_send,
    north_send,
    west_recv,
    east_recv,
    south_recv,
    north_recv,
    zbuf,
    pbuf,
    alpha_co,
    gamma_co,
    last_co,
    line_count,
    row_count,
    ghost_west,
    ghost_east,
    in_sem,
    a2a_send_sem,
    a2a_recv_sem,
    halo_send_sem,
    halo_recv_sem,
    z_send_sem,
    z_recv_sem,
    p_send_sem,
    p_recv_sem,
):
    ny, nzh, nx, nc = DIMS
    nz = nzh * NG
    np_ = ny * nx * nc
    t = lax.axis_index("tile")
    g = lax.axis_index("grp")
    c = lax.rem(t, nc)
    x = lax.rem(lax.div(t, nc), nx)
    zh = lax.rem(lax.div(t, nc * nx), nzh)
    y = lax.div(t, nc * nx * nzh)
    z = zh * NG + g
    p = (y * nx + x) * nc + c

    def tile_of(y_, zh_, x_, c_):
        return ((y_ * nzh + zh_) * nx + x_) * nc + c_

    z_part = [lax.rem(zh + dz, nzh) * (nx * nc) for dz in range(nzh)]
    z_order = sorted(range(nzh), key=lambda dz: -min(dz, nzh - dz))

    def plane_base(r):
        dc = lax.rem(r, nc)
        dx = lax.rem(lax.div(r, nc), nx)
        dy = lax.div(r, nc * nx)
        low = lax.rem(x + dx, nx) * nc + lax.rem(c + dc, nc)
        return lax.rem(y + dy, ny) * (nzh * nx * nc) + low

    def each_tile(low, high, act):
        if low == 0:
            base = plane_base(0)
            for dz in z_order[:-1]:
                act(base + z_part[dz])

        def some(r, _):
            base = plane_base(r)
            for dz in z_order:
                act(base + z_part[dz])
            return 0

        lax.fori_loop(max(low, 1), high, some, 0)

    plane_here = plane_base(0)

    def each_z(first, act):
        if first == 0:
            for dz in z_order[:-1]:
                act(plane_here + z_part[dz], g)

        def some(dg, _):
            g2 = lax.rem(g + dg, NG)
            for dz in z_order:
                act(plane_here + z_part[dz], g2)
            return 0

        lax.fori_loop(1, NG, some, 0)

    barrier = pltpu.get_barrier_semaphore()

    def greet(tile, grp):
        pl.semaphore_signal(barrier, inc=1, device_id=(tile, grp), device_id_type=MESH)

    each_z(1, greet)
    each_tile(0, np_, lambda tile: greet(tile, g))
    pairs = (
        (kel_hbm, kel),
        (longwave_hbm, longwave),
        (shortwave_hbm, shortwave),
        (link_hbm, link),
        (sh_hbm, sh),
        (fv_hbm, fv.at[pl.ds(0, LV)]),
    )
    loads = [pltpu.make_async_copy(src, dst, in_sem.at[i]) for i, (src, dst) in enumerate(pairs)]
    for load in loads:
        load.start()
    for load in loads:
        load.wait()

    def wait_lines(sem):
        pltpu.make_async_copy(line_count, line_count, sem).wait()

    def wait_rows(sem):
        rows = row_count.at[pl.ds(0, nz - 1)]
        pltpu.make_async_copy(rows, rows, sem).wait()

    def a2a_start(src, dst, which, low, high):
        def send(peer):
            pltpu.make_async_remote_copy(
                src_ref=src.at[pl.ds(peer, 1), :],
                dst_ref=dst.at[pl.ds(t, 1), :],
                send_sem=a2a_send_sem.at[which],
                recv_sem=a2a_recv_sem.at[which],
                device_id=(peer, g),
                device_id_type=MESH,
            ).start()

        each_tile(low, high, send)

    def a2a_wait(which):
        wait_lines(a2a_recv_sem.at[which])

    def a2a_drain(which):
        wait_lines(a2a_send_sem.at[which])

    lane = iota((PX, CY), 1)
    row8 = iota((PX, CY), 0)

    def pack_row(values):
        rows = [jnp.sum(v, axis=0, keepdims=True) for v in values]
        rows = rows + [jnp.zeros((1, CY), F32)] * (NM - len(rows))
        sums = jnp.sum(jnp.concatenate(rows, axis=0), axis=1, keepdims=True)
        diag = iota((NM, 128), 0) == iota((NM, 128), 1)
        return jnp.sum(jnp.where(diag, sums, 0.0), axis=0, keepdims=True)

    def gather_start(which, row):
        buf = zbuf.at[which]
        buf[pl.ds(z, 1), :] = row

        def send(tile, grp):
            pltpu.make_async_remote_copy(
                src_ref=buf.at[pl.ds(z, 1), :],
                dst_ref=buf.at[pl.ds(z, 1), :],
                send_sem=z_send_sem.at[which],
                recv_sem=z_recv_sem.at[which],
                device_id=(tile, grp),
                device_id_type=MESH,
            ).start()

        each_z(0, send)

    def gather_middle(which):
        buf = zbuf.at[which]
        wait_rows(z_recv_sem.at[which])
        value = buf[...]
        ln = iota((nz, 128), 1)
        mine = lax.rem(ln, nz) == iota((nz, 128), 0)
        packed = []
        for r in range(NM // 8):
            spread = jnp.take_along_axis(value, lax.rem(r * 8 + lax.div(ln, nz), 128), axis=1)
            packed.append(jnp.sum(jnp.where(mine, spread, 0.0), axis=0, keepdims=True))
        pbuf[which, pl.ds(p, 1)] = jnp.concatenate(packed, axis=0)[None]
        dst = pbuf.at[which]

        def send(r, _):
            pltpu.make_async_remote_copy(
                src_ref=dst.at[pl.ds(p, 1)],
                dst_ref=dst.at[pl.ds(p, 1)],
                send_sem=p_send_sem.at[which],
                recv_sem=p_recv_sem.at[which],
                device_id=(plane_base(r) + z_part[0], g),
                device_id_type=MESH,
            ).start()
            return 0

        lax.fori_loop(1, np_, send, 0)

    def gather_end(which, count):
        rows = pbuf.at[which, pl.ds(0, np_ - 1)]
        pltpu.make_async_copy(rows, rows, p_recv_sem.at[which]).wait()
        parts = [pbuf[which, :, r, :] for r in range(NM // 8)]
        parts.append(jnp.zeros((128 - np_ * (NM // 8), 128), F32))
        flat = jnp.concatenate(parts, axis=0).T
        ln = iota((128, 128), 1)
        rw = iota((128, 128), 0)
        t_p = (lax.rem(lax.div(ln, nc * nx * nzh), ny) * nx * nc) + lax.rem(ln, nx * nc)
        t_zh = lax.rem(lax.div(ln, nc * nx), nzh)
        keep = lax.div(lax.rem(rw, nz), NG) == t_zh
        found = []
        for r in range(NM // 8):
            if len(found) >= count:
                break
            got = jnp.take_along_axis(flat, t_p + r * np_, axis=1)
            got = jnp.where(keep, got, 0.0)
            for m in range(8):
                if len(found) >= count:
                    break
                block = got[m * nz : (m + 1) * nz, :NT]
                acc = block[0:NG]
                for b in range(1, nzh):
                    acc = acc + block[b * NG : (b + 1) * NG]
                found.append(jnp.concatenate([acc, jnp.zeros((GP - NG, NT), F32)], axis=0))
        return found

    def gather_drain(which):
        wait_rows(z_send_sem.at[which])
        rows = pbuf.at[which, pl.ds(0, np_ - 1)]
        pltpu.make_async_copy(rows, rows, p_send_sem.at[which]).wait()

    zeros = jnp.zeros((PX, CY), F32)
    latitude = ((g * CY + t).astype(F32) + 0.5) / float(CY * NG) - 0.5
    mu10 = 10.0 * jnp.cos(jnp.full((PX, CY), latitude * (math.pi / 2) - 0.4, F32))

    def emission(k):
        square = kel[k] * kel[k]
        return square * square

    def both_passes(k, carry):
        flux_down, flux_up, sun, acc = carry
        em = emission(k)
        trans = jnp.exp(jnp.full((PX, CY), -longwave[k], F32))
        absorbed = 1.0 - trans
        sun_trans = jnp.exp(jnp.full((PX, CY), -shortwave[k], F32))
        raw = absorbed * (flux_down - 2.0 * em) + mu10 * (sun * (1.0 - sun_trans))
        down[k] = raw
        flux_down = trans * flux_down + absorbed * em
        sun = sun * sun_trans
        k2 = LV - 1 - k
        em2 = emission(k2)
        trans2 = jnp.exp(jnp.full((PX, CY), -longwave[k2], F32))
        absorbed2 = 1.0 - trans2
        raw2 = absorbed2 * flux_up
        upw[k2] = raw2
        flux_up = trans2 * flux_up + absorbed2 * em2
        return flux_down, flux_up, sun, acc + (raw + raw2)

    carry = blocked(LV, both_passes, (zeros, emission(LV - 1), jnp.ones((PX, CY), F32), zeros))
    mean = carry[3] * (1.0 / LV)
    for k in range(LV, LP):
        fv[k] = zeros
        smooth1[k] = zeros
        down[k] = zeros
        upw[k] = zeros
        res[k] = zeros
    for ch in range(NCH):
        lv = slice(ch * 16, (ch + 1) * 16)
        heat = down[lv] + upw[lv] - mean[None]
        down[lv] = heat
        hs[:, ch * 128 : (ch + 1) * 128] = heat.reshape(16 * PX, CY).T

    def lines_of(field, dst):
        for ch in range(NCH):
            dst[:, ch * 128 : (ch + 1) * 128] = (
                field[ch * 16 : (ch + 1) * 16].reshape(16 * PX, CY).T
            )

    def columns_of(src, ch):
        top = min(LV, (ch + 1) * 16)
        block = src[:, ch * 128 : (ch + 1) * 128].T.reshape(16, PX, CY)
        return slice(ch * 16, top), block[: top - ch * 16]

    lines_of(fv, fs)

    def factor(k, carry):
        link_above, inv_above = carry
        here = jnp.where(k < LV - 1, link[jnp.minimum(k, LV - 2)], 0.0)
        here = jnp.full((PX, CY), here, F32)
        low = link_above * inv_above
        inv = 1.0 / (4.0 + here + link_above - link_above * low)
        lco[k] = low
        cco[k] = inv
        return here, inv

    blocked(LV, factor, (zeros, zeros))
    lco[LV] = zeros

    def shift_sums(k, carry):
        v = sh[k]
        return carry[0] + v, carry[1] + v * v

    sh_sum, sh_sq = blocked(LV, shift_sums, (zeros, zeros))
    edge_w = row8 == 0
    edge_e = row8 == PX - 1
    edge_s = lane == 0
    edge_n = lane == CY - 1

    def edges(v):
        return [jnp.where(m, v, 0.0) for m in (edge_w, edge_e, edge_s, edge_n)]

    shift_row = pack_row([sh_sum, sh_sq] + edges(sh_sum))

    def column_solve(source, dst):
        def forward(k, above):
            value = source(k) + lco[k] * above
            dst[k] = value
            return value

        blocked(LV, forward, zeros)

        def backward(k, carry):
            below, to_south, to_north = carry
            value = cco[k] * dst[k] + lco[k + 1] * below
            dst[k] = value
            to_south = jnp.where(lane == k, roll(value, k, 1), to_south)
            to_north = jnp.where(lane == k, roll(value, lax.rem(k + 1, CY), 1), to_north)
            return value, to_south, to_north

        return blocked(LV, backward, (zeros, zeros, zeros), reverse=True)

    def halo_copies(n):
        left = (lax.rem(t + NT - 1, NT), g)
        right = (lax.rem(t + 1, NT), g)
        below = (t, lax.rem(g + NG - 1, NG))
        above = (t, lax.rem(g + 1, NG))
        table = (
            (west_send, east_recv, left),
            (east_send, west_recv, right),
            (south_send, north_recv, below),
            (north_send, south_recv, above),
        )
        return [
            pltpu.make_async_remote_copy(
                src_ref=src.at[n],
                dst_ref=dst.at[n],
                send_sem=halo_send_sem.at[n, i],
                recv_sem=halo_recv_sem.at[n, i],
                device_id=device,
                device_id_type=MESH,
            )
            for i, (src, dst, device) in enumerate(table)
        ]

    def halo_fill(n, field, rims):
        west_send[n] = field[0:LV, 0, :]
        east_send[n] = field[0:LV, PX - 1, :]
        south_send[n] = rims[1]
        north_send[n] = rims[2]

    def halo_start(n):
        copies = halo_copies(n)
        for copy in copies:
            copy.start()
        return copies

    def plain_solve(field, dst):
        def forward(k, above):
            value = field[k] + lco[k] * above
            dst[k] = value
            return value

        blocked(LV, forward, zeros)

        def backward(k, below):
            value = cco[k] * dst[k] + lco[k + 1] * below
            dst[k] = value
            return value

        blocked(LV, backward, zeros, reverse=True)

    shift_rims = column_solve(lambda k: sh[k], shift_solve)
    halo_fill(2, shift_solve, shift_rims)

    pl.semaphore_wait(barrier, NT - 1 + (NG - 1) * nzh)

    gather_start(0, shift_row)
    a2a_start(hs, hr, 0, 0, np_)
    hr[pl.ds(t, 1), :] = hs[pl.ds(t, 1), :]
    fr[pl.ds(t, 1), :] = fs[pl.ds(t, 1), :]
    halos2 = halo_start(2)
    gather_middle(0)

    mass, m_ss, m_sw, m_se, m_sso, m_sn = gather_end(0, 6)
    grow = iota((GP, NT), 0)
    gcol = iota((GP, NT), 1)
    live_s = ((grow > 0) & (grow < NG)).astype(F32)
    live_n = (grow < NG - 1).astype(F32)
    diagonal = mass + 2.0 * LV * CY + LV * PX * (live_s + live_n)
    couple = float(LV * CY)
    b_co = []
    a_co = []
    for j in range(NG):
        entry = jnp.where(grow == j, diagonal, 0.0)
        near = (grow == j - 1) | (grow == j + 1)
        entry = jnp.where(near & (grow < NG), -float(LV * PX), entry)
        b_co.append(entry)
        a_co.append(jnp.where(grow == j, -couple, 0.0))

    def reduce_step(step, carry):
        hop, a_, b_, c_ = carry
        back = NT - hop
        binv = inverse4(b_)
        alpha = matmul4(a_, [roll(v, hop, 1) for v in binv])
        gamma = matmul4(c_, [roll(v, back, 1) for v in binv])
        alpha = [-v for v in alpha]
        gamma = [-v for v in gamma]
        a_m = [roll(v, hop, 1) for v in a_]
        c_m = [roll(v, hop, 1) for v in c_]
        a_p = [roll(v, back, 1) for v in a_]
        c_p = [roll(v, back, 1) for v in c_]
        ac = matmul4(alpha, c_m)
        ga = matmul4(gamma, a_p)
        b_ = [b_[j] + ac[j] + ga[j] for j in range(NG)]
        a_ = matmul4(alpha, a_m)
        c_ = matmul4(gamma, c_p)
        for j in range(NG):
            alpha_co[step, j] = alpha[j]
            gamma_co[step, j] = gamma[j]
        return hop * 2, tuple(a_), tuple(b_), tuple(c_)

    steps = int(math.log2(NT))
    _, a_f, b_f, c_f = lax.fori_loop(
        0, steps, reduce_step, (jnp.int32(1), tuple(a_co), tuple(b_co), tuple(a_co))
    )
    last = inverse4([a_f[j] + b_f[j] + c_f[j] for j in range(NG)])
    for j in range(NG):
        last_co[j] = last[j]

    def coarse_solve(rhs):
        for step in range(steps):
            hop = 1 << step
            low = roll(rhs, hop, 1)
            high = roll(rhs, NT - hop, 1)
            rhs = (
                rhs
                + matvec4([alpha_co[step, j] for j in range(NG)], low)
                + matvec4([gamma_co[step, j] for j in range(NG)], high)
            )
        return matvec4([last_co[j] for j in range(NG)], rhs)

    def differences(e):
        return (
            e - roll(e, 1, 1),
            e - roll(e, NT - 1, 1),
            live_s * (e - roll(e, 1, 0)),
            live_n * (e - roll(e, GP - 1, 0)),
        )

    mine = (grow == g) & (gcol == t)

    def own(v):
        return total(jnp.where(mine, v, 0.0))

    def rim_of(west, east, south, north):
        return (
            jnp.where(edge_w, west, 0.0)
            + jnp.where(edge_e, east, 0.0)
            + jnp.where(edge_s, south, 0.0)
            + jnp.where(edge_n, north, 0.0)
        )

    long_rim = float(LV * CY)
    short_rim = float(LV * PX)
    corner = float(LV)
    m_shift = (m_sw, m_se, m_sso, m_sn)

    def own_square(e, w):
        cross = (w[0] + w[1]) * (w[2] + w[3])
        value = e * e * m_ss + long_rim * (w[0] * w[0] + w[1] * w[1])
        value = value + short_rim * (w[2] * w[2] + w[3] * w[3]) + 2.0 * corner * cross
        for i in range(4):
            value = value + 2.0 * e * w[i] * m_shift[i]
        return value

    def against(e, w, with_shift, with_edges):
        value = e * with_shift
        for i in range(4):
            value = value + w[i] * with_edges[i]
        return value

    inner_s = edge_s & (g > 0)
    outer_s = edge_s & (g == 0)
    inner_n = edge_n & (g < NG - 1)
    outer_n = edge_n & (g == NG - 1)

    def image_level(v, r, k, west_in, east_in, south_in, north_in):
        west = jnp.where(edge_w, west_in[pl.ds(k, 1), :], roll(v, 1, 0))
        east = jnp.where(edge_e, east_in[pl.ds(k, 1), :], roll(v, PX - 1, 0))
        south = jnp.where(inner_s, roll(south_in, lax.rem(CY - k, CY), 1), roll(v, 1, 1))
        south = jnp.where(outer_s, v, south)
        north = jnp.where(inner_n, roll(north_in, CY - 1 - k, 1), roll(v, CY - 1, 1))
        north = jnp.where(outer_n, v, north)
        return r - ((west + east) + (south + north)) + sh[k] * v

    a2a_wait(0)
    for ch in range(NCH):
        lv, block = columns_of(hr, ch)
        res[lv] = fv[lv] + block

    half = np_ // 2
    rims = column_solve(lambda k: res[k], smooth0)
    halo_fill(0, smooth0, rims)
    halos0 = halo_start(0)
    a2a_start(fs, fr, 1, 0, half)
    for copy in halos0:
        copy.wait_recv()
    south_in = south_recv[0]
    north_in = north_recv[0]

    def moments0(k, carry):
        r_sum, q_sum, rq, rs, qq, qs = carry
        r = res[k]
        q = image_level(
            smooth0[k], r, k, west_recv.at[0], east_recv.at[0], south_in, north_in
        )
        image[k] = q
        s = sh[k]
        return r_sum + r, q_sum + q, rq + r * q, rs + r * s, qq + q * q, qs + q * s

    r_sum, q_sum, rq, rs, qq, qs = blocked(LV, moments0, (zeros,) * 6)
    gather_start(1, pack_row([r_sum - q_sum, rq, rs, qq, qs] + edges(r_sum) + edges(q_sum)))
    image_rims = column_solve(lambda k: image[k], image_solve)
    halo_fill(1, image_solve, image_rims)
    halos1 = halo_start(1)
    a2a_start(fs, fr, 1, half, np_)
    gather_middle(1)
    got = gather_end(1, 13)
    e0 = coarse_solve(got[0])
    w0 = differences(e0)
    m_rq, m_rs, m_qq, m_qs = got[1:5]
    m_re = got[5:9]
    m_qe = got[9:13]
    projection = total(m_rq + against(e0, w0, m_rs, m_re))
    norm0 = total(m_qq + 2.0 * against(e0, w0, m_qs, m_qe) + own_square(e0, w0))
    step0 = projection / norm0
    left_over = projection - step0 * norm0
    i_s = m_qs + against(e0, w0, m_ss, m_shift)
    i_e = (
        m_qe[0] + e0 * m_sw + long_rim * w0[0] + corner * (w0[2] + w0[3]),
        m_qe[1] + e0 * m_se + long_rim * w0[1] + corner * (w0[2] + w0[3]),
        m_qe[2] + e0 * m_sso + short_rim * w0[2] + corner * (w0[0] + w0[1]),
        m_qe[3] + e0 * m_sn + short_rim * w0[3] + corner * (w0[0] + w0[1]),
    )
    at_west = (grow == g) & (gcol == lax.rem(t + NT - 1, NT))
    at_east = (grow == g) & (gcol == lax.rem(t + 1, NT))
    at_south = (grow == g - 1) & (gcol == t)
    at_north = (grow == g + 1) & (gcol == t)
    wanted = [(m, e0) for m in (mine, at_west, at_east, at_south, at_north)]
    wanted = wanted + [(mine, v) for v in w0]
    wanted = wanted + [(at_west, w0[i]) for i in (1, 2, 3)]
    wanted = wanted + [(at_east, w0[i]) for i in (0, 2, 3)]
    wanted = wanted + [(at_south, w0[i]) for i in (3, 0, 1)]
    wanted = wanted + [(at_north, w0[i]) for i in (2, 0, 1)]
    found = [jnp.sum(jnp.where(m, v, 0.0), axis=0, keepdims=True) for m, v in wanted]
    found = found + [jnp.zeros((1, NT), F32)] * (24 - len(found))
    found = jnp.sum(jnp.concatenate(found, axis=0), axis=1, keepdims=True)
    found = [found[i : i + 1] for i in range(21)]
    e0_own, e_west, e_east, e_south, e_north = found[0:5]
    rim0 = rim_of(*found[5:9])
    lane1 = iota((1, CY), 1)
    row1 = iota((PX, 1), 0)

    def rim_row(f):
        return f[0] + jnp.where(lane1 == 0, f[1], 0.0) + jnp.where(lane1 == CY - 1, f[2], 0.0)

    def rim_col(f):
        return f[0] + jnp.where(row1 == 0, f[1], 0.0) + jnp.where(row1 == PX - 1, f[2], 0.0)

    for copy in halos2 + halos1:
        copy.wait_recv()

    def ghost(recv, e, rim):
        return recv[0] - step0 * (recv[1] + e * recv[2] + 0.25 * rim)

    ghost_west[...] = ghost(west_recv, e_west, rim_row(found[9:12]))
    ghost_east[...] = ghost(east_recv, e_east, rim_row(found[12:15]))
    ghost_south = ghost(south_recv, e_south, rim_col(found[15:18]))
    ghost_north = ghost(north_recv, e_north, rim_col(found[18:21]))

    quarter_rim = 0.25 * rim0

    def moments1(k, carry):
        r_sum, q_sum, rq, rs, qq, qs, iq = carry
        s = sh[k]
        q0 = image[k] + s * e0_own + rim0
        r = res[k] - step0 * q0
        v = smooth0[k] - step0 * (image_solve[k] + e0_own * shift_solve[k] + quarter_rim)
        smooth1[k] = v
        q = image_level(v, r, k, ghost_west, ghost_east, ghost_south, ghost_north)
        return (
            r_sum + r,
            q_sum + q,
            rq + r * q,
            rs + r * s,
            qq + q * q,
            qs + q * s,
            iq + q0 * q,
        )

    r_sum, q_sum, rq, rs, qq, qs, iq = blocked(LV, moments1, (zeros,) * 7)
    gather_start(2, pack_row([r_sum - q_sum, rq, rs, qq, qs] + edges(r_sum) + edges(q_sum) + [iq]))
    lines_of(smooth1, xs)
    a2a_start(xs, xr, 2, 0, half)
    xr[pl.ds(t, 1), :] = xs[pl.ds(t, 1), :]

    a2a_wait(1)
    for ch in range(NCH):
        lv, block = columns_of(fr, ch)
        down[lv] = down[lv] + block
    plain_solve(down, upw)

    gather_middle(2)
    a2a_start(xs, xr, 2, half, np_)
    got = gather_end(2, 14)
    e1 = coarse_solve(got[0])
    w1 = differences(e1)
    m_rq, m_rs, m_qq, m_qs = got[1:5]
    m_re = got[5:9]
    m_qe = got[9:13]
    crossing = total(got[13] + against(e1, w1, i_s, i_e))
    projection1 = total(m_rq + against(e1, w1, m_rs, m_re))
    square1 = total(m_qq + 2.0 * against(e1, w1, m_qs, m_qe) + own_square(e1, w1))
    weight = crossing / norm0
    norm1 = square1 - weight * crossing
    step1 = (projection1 - weight * left_over) / norm1
    scale0 = step0 - step1 * weight
    block_part = scale0 * e0 + step1 * e1
    constant = own(block_part)
    by_tile = jnp.sum(jnp.where(grow == g, block_part, 0.0), axis=0, keepdims=True)

    def finish(k, _):
        out_field[k] = scale0 * smooth0[k] + step1 * smooth1[k] + constant
        return 0

    blocked(LV, finish, 0)

    a2a_wait(2)
    for ch in range(NCH):
        lv, block = columns_of(xr, ch)
        out_rad[lv] = scale0 * upw[lv] + step1 * block + by_tile[None]

    for which in range(3):
        a2a_drain(which)
        gather_drain(which)
    for copy in halos0 + halos1 + halos2:
        copy.wait_send()


def per_device(fv, sh, link, kel, longwave, shortwave):
    vmem = pl.BlockSpec(memory_space=pltpu.VMEM)
    hbm = pl.BlockSpec(memory_space=pltpu.HBM)
    field = jax.ShapeDtypeStruct((LV, PX, CY), F32)
    np_ = DIMS[0] * DIMS[2] * DIMS[3]
    steps = int(math.log2(NT))
    padded = pltpu.VMEM((LP, PX, CY), F32)
    whole = pltpu.VMEM((LV, PX, CY), F32)
    lines = pltpu.VMEM((NT, LP * PX), F32)
    rims = pltpu.VMEM((3, LV, CY), F32)
    corners = pltpu.VMEM((3, PX, CY), F32)
    dma = pltpu.SemaphoreType.DMA
    return pl.pallas_call(
        kernel,
        out_shape=(field, field),
        in_specs=[hbm] * 6,
        out_specs=(vmem, vmem),
        scratch_shapes=[padded, whole, whole]
        + [pltpu.SMEM((LV - 1,), F32), pltpu.SMEM((LV,), F32), pltpu.SMEM((LV,), F32)]
        + [padded] * 10
        + [lines] * 6
        + [rims, rims, corners, corners, rims, rims, corners, corners]
        + [
            pltpu.VMEM((3, DIMS[1] * NG, 128), F32),
            pltpu.VMEM((3, np_, NM // 8, 128), F32),
            pltpu.VMEM((steps, NG, GP, NT), F32),
            pltpu.VMEM((steps, NG, GP, NT), F32),
            pltpu.VMEM((NG, GP, NT), F32),
            pltpu.VMEM((NT - 1, 1, LP * PX), F32),
            pltpu.VMEM((DIMS[1] * NG, 1, 128), F32),
            pltpu.VMEM((LV, CY), F32),
            pltpu.VMEM((LV, CY), F32),
            dma((6,)),
            dma((3,)),
            dma((3,)),
            dma((3, 4)),
            dma((3, 4)),
            dma((3,)),
            dma((3,)),
            dma((3,)),
            dma((3,)),
        ],
        compiler_params=pltpu.CompilerParams(
            collective_id=0, has_side_effects=True, vmem_limit_bytes=67043328
        ),
        name="step",
    )(fv, sh, kel, link, longwave, shortwave)


def solution(mesh):
    spread = P(None, "tile", "grp")
    columns = P(None, None, ("tile", "grp"))
    return jax.shard_map(
        per_device,
        mesh=mesh,
        in_specs=(spread, spread, P(), columns, P(), P()),
        out_specs=(spread, columns),
        check_vma=False,
    )
```

```python
import math

import jax
import jax.numpy as jnp
from jax import lax
from jax.experimental import pallas as pl
from jax.experimental.pallas import tpu as pltpu
from jax.sharding import PartitionSpec as P

LV = 70
PX = 8
CY = 128
NG = 4
DIMS = (4, 4, 4, 2)
NT = 128
LP = 80
NCH = LP // 16
UNROLL = 10
NM = 16
GP = 8
F32 = jnp.float32
MESH = pl.DeviceIdType.MESH


def iota(shape, dim):
    return lax.broadcasted_iota(jnp.int32, shape, dim)


def roll(value, shift, axis):
    return pltpu.roll(value, shift, axis)


def blocked(levels, body, init, reverse=False):
    def trip(b, carry):
        for j in range(UNROLL):
            k = b * UNROLL + j
            carry = body(levels - 1 - k if reverse else k, carry)
        return carry

    return lax.fori_loop(0, levels // UNROLL, trip, init)


def total(value):
    return jnp.sum(jnp.sum(value, axis=0, keepdims=True), axis=1, keepdims=True)


def matmul4(left, right):
    out = []
    for j in range(NG):
        term = left[0] * right[j][0:1, :]
        for l in range(1, NG):
            term = term + left[l] * right[j][l : l + 1, :]
        out.append(term)
    return out


def inverse4(columns):
    columns = list(columns)
    row = iota((GP, NT), 0)
    for k in range(NG):
        pivot = 1.0 / columns[k][k : k + 1, :]
        for j in range(NG):
            if j != k:
                scaled = columns[j][k : k + 1, :] * pivot
                columns[j] = jnp.where(row == k, scaled, columns[j] - columns[k] * scaled)
        columns[k] = jnp.where(row == k, pivot, -columns[k] * pivot)
    return columns


def matvec4(columns, vector):
    out = columns[0] * vector[0:1, :]
    for l in range(1, NG):
        out = out + columns[l] * vector[l : l + 1, :]
    return out


def kernel(
    fv_hbm,
    sh_hbm,
    kel_hbm,
    link_hbm,
    longwave_hbm,
    shortwave_hbm,
    out_field,
    out_rad,
    fv,
    sh,
    kel,
    link,
    longwave,
    shortwave,
    down,
    upw,
    lco,
    cco,
    res,
    smooth0,
    smooth1,
    image,
    shift_solve,
    image_solve,
    hs,
    mid,
    hr,
    fs,
    fr,
    xs,
    xr,
    west_send,
    east_send,
    south_send,
    north_send,
    west_recv,
    east_recv,
    south_recv,
    north_recv,
    zbuf,
    pbuf,
    alpha_co,
    gamma_co,
    last_co,
    line_count,
    row_count,
    ghost_west,
    ghost_east,
    turn_send_sem,
    turn_recv_sem,
    turn_own_sem,
    own_sem,
    in_sem,
    a2a_send_sem,
    a2a_recv_sem,
    halo_send_sem,
    halo_recv_sem,
    z_send_sem,
    z_recv_sem,
    p_send_sem,
    p_recv_sem,
):
    ny, nzh, nx, nc = DIMS
    nz = nzh * NG
    np_ = ny * nx * nc
    t = lax.axis_index("tile")
    g = lax.axis_index("grp")
    c = lax.rem(t, nc)
    x = lax.rem(lax.div(t, nc), nx)
    zh = lax.rem(lax.div(t, nc * nx), nzh)
    y = lax.div(t, nc * nx * nzh)
    z = zh * NG + g
    p = (y * nx + x) * nc + c

    def tile_of(y_, zh_, x_, c_):
        return ((y_ * nzh + zh_) * nx + x_) * nc + c_

    z_part = [lax.rem(zh + dz, nzh) * (nx * nc) for dz in range(nzh)]
    z_order = sorted(range(nzh), key=lambda dz: -min(dz, nzh - dz))

    def plane_base(r):
        dc = lax.rem(r, nc)
        dx = lax.rem(lax.div(r, nc), nx)
        dy = lax.div(r, nc * nx)
        low = lax.rem(x + dx, nx) * nc + lax.rem(c + dc, nc)
        return lax.rem(y + dy, ny) * (nzh * nx * nc) + low

    def each_tile(low, high, act):
        if low == 0:
            base = plane_base(0)
            for dz in z_order[:-1]:
                act(base + z_part[dz])

        def some(r, _):
            base = plane_base(r)
            for dz in z_order:
                act(base + z_part[dz])
            return 0

        lax.fori_loop(max(low, 1), high, some, 0)

    def each_plane(act):
        def one(r, _):
            act(r)
            return 0

        lax.fori_loop(1, np_, one, 0)

    plane_here = plane_base(0)

    def each_z(first, act):
        if first == 0:
            for dz in z_order[:-1]:
                act(plane_here + z_part[dz], g)

        def some(dg, _):
            g2 = lax.rem(g + dg, NG)
            for dz in z_order:
                act(plane_here + z_part[dz], g2)
            return 0

        lax.fori_loop(1, NG, some, 0)

    barrier = pltpu.get_barrier_semaphore()

    def greet(tile, grp):
        pl.semaphore_signal(barrier, inc=1, device_id=(tile, grp), device_id_type=MESH)

    ring_before = lax.rem(t + NT - 1, NT)
    ring_after = lax.rem(t + 1, NT)
    each_z(0, greet)
    each_plane(lambda r: greet(plane_base(r) + z_part[0], g))
    greet(ring_before, g)
    greet(ring_after, g)
    pairs = (
        (kel_hbm, kel),
        (longwave_hbm, longwave),
        (shortwave_hbm, shortwave),
        (link_hbm, link),
        (sh_hbm, sh),
        (fv_hbm, fv.at[pl.ds(0, LV)]),
    )
    loads = [pltpu.make_async_copy(src, dst, in_sem.at[i]) for i, (src, dst) in enumerate(pairs)]
    for load in loads:
        load.start()
    for load in loads:
        load.wait()

    def wait_lines(sem):
        pltpu.make_async_copy(line_count, line_count, sem).wait()

    def wait_rows(sem):
        rows = row_count.at[pl.ds(0, nz - 1)]
        pltpu.make_async_copy(rows, rows, sem).wait()

    def a2a_start(src, dst, which, low, high):
        def send(peer):
            pltpu.make_async_remote_copy(
                src_ref=src.at[pl.ds(peer, 1)],
                dst_ref=dst.at[pl.ds(t, 1)],
                send_sem=a2a_send_sem.at[which],
                recv_sem=a2a_recv_sem.at[which],
                device_id=(peer, g),
                device_id_type=MESH,
            ).start()

        each_tile(low, high, send)

    nxc = nx * nc
    xc = lax.rem(t, nxc)

    def turn_rows(dy):
        return lax.rem(y + dy, ny)

    def turn_start():
        for dy in range(ny):
            y2 = turn_rows(dy)
            for dz in z_order[:-1]:
                peer = plane_here + z_part[dz]
                zh2 = lax.rem(zh + dz, nzh)
                pltpu.make_async_remote_copy(
                    src_ref=hs.at[pl.ds((y2 * nzh + zh2) * nxc, nxc)],
                    dst_ref=mid.at[zh, pl.ds(y2 * nxc, nxc)],
                    send_sem=turn_send_sem,
                    recv_sem=turn_recv_sem.at[dy],
                    device_id=(peer, g),
                    device_id_type=MESH,
                ).start()
            pltpu.make_async_copy(
                hs.at[pl.ds((y2 * nzh + zh) * nxc, nxc)],
                mid.at[zh, pl.ds(y2 * nxc, nxc)],
                turn_own_sem.at[dy],
            ).start()

    def line_wait(count, sem):
        part = line_count.at[pl.ds(0, count)]
        pltpu.make_async_copy(part, part, sem).wait()

    def turn_middle():
        for dy in range(ny):
            y2 = turn_rows(dy)
            line_wait((nzh - 1) * nxc, turn_recv_sem.at[dy])
            line_wait(nxc, turn_own_sem.at[dy])

            def one(r, _, y2=y2):
                xc2 = lax.rem(xc + r, nxc)
                pltpu.make_async_remote_copy(
                    src_ref=mid.at[:, y2 * nxc + xc2],
                    dst_ref=hr.at[y, :, xc],
                    send_sem=a2a_send_sem.at[0],
                    recv_sem=a2a_recv_sem.at[0],
                    device_id=((y2 * nzh + zh) * nxc + xc2, g),
                    device_id_type=MESH,
                ).start()
                return 0

            lax.fori_loop(1 if dy == 0 else 0, nxc, one, 0)
        own_copy = pltpu.make_async_copy(mid.at[:, p], hr.at[y, :, xc], own_sem)
        own_copy.start()
        own_copy.wait()

    def a2a_wait(which):
        wait_lines(a2a_recv_sem.at[which])

    def a2a_drain(which):
        wait_lines(a2a_send_sem.at[which])

    lane = iota((PX, CY), 1)
    row8 = iota((PX, CY), 0)

    def pack_row(values):
        rows = [jnp.sum(v, axis=0, keepdims=True) for v in values]
        rows = rows + [jnp.zeros((1, CY), F32)] * (NM - len(rows))
        sums = jnp.sum(jnp.concatenate(rows, axis=0), axis=1, keepdims=True)
        diag = iota((NM, 128), 0) == iota((NM, 128), 1)
        return jnp.sum(jnp.where(diag, sums, 0.0), axis=0, keepdims=True)

    def gather_start(which, row):
        buf = zbuf.at[which]
        buf[pl.ds(z, 1), :] = row

        def send(tile, grp):
            pltpu.make_async_remote_copy(
                src_ref=buf.at[pl.ds(z, 1), :],
                dst_ref=buf.at[pl.ds(z, 1), :],
                send_sem=z_send_sem.at[which],
                recv_sem=z_recv_sem.at[which],
                device_id=(tile, grp),
                device_id_type=MESH,
            ).start()

        each_z(0, send)

    def gather_middle(which):
        buf = zbuf.at[which]
        wait_rows(z_recv_sem.at[which])
        value = buf[...]
        ln = iota((nz, 128), 1)
        mine = lax.rem(ln, nz) == iota((nz, 128), 0)
        packed = []
        for r in range(NM // 8):
            spread = jnp.take_along_axis(value, lax.rem(r * 8 + lax.div(ln, nz), 128), axis=1)
            packed.append(jnp.sum(jnp.where(mine, spread, 0.0), axis=0, keepdims=True))
        pbuf[which, pl.ds(p, 1)] = jnp.concatenate(packed, axis=0)[None]
        dst = pbuf.at[which]

        def send(r, _):
            pltpu.make_async_remote_copy(
                src_ref=dst.at[pl.ds(p, 1)],
                dst_ref=dst.at[pl.ds(p, 1)],
                send_sem=p_send_sem.at[which],
                recv_sem=p_recv_sem.at[which],
                device_id=(plane_base(r) + z_part[0], g),
                device_id_type=MESH,
            ).start()
            return 0

        lax.fori_loop(1, np_, send, 0)

    def gather_end(which, count):
        rows = pbuf.at[which, pl.ds(0, np_ - 1)]
        pltpu.make_async_copy(rows, rows, p_recv_sem.at[which]).wait()
        parts = [pbuf[which, :, r, :] for r in range(NM // 8)]
        parts.append(jnp.zeros((128 - np_ * (NM // 8), 128), F32))
        flat = jnp.concatenate(parts, axis=0).T
        ln = iota((128, 128), 1)
        rw = iota((128, 128), 0)
        t_p = (lax.rem(lax.div(ln, nc * nx * nzh), ny) * nx * nc) + lax.rem(ln, nx * nc)
        t_zh = lax.rem(lax.div(ln, nc * nx), nzh)
        keep = lax.div(lax.rem(rw, nz), NG) == t_zh
        found = []
        for r in range(NM // 8):
            if len(found) >= count:
                break
            got = jnp.take_along_axis(flat, t_p + r * np_, axis=1)
            got = jnp.where(keep, got, 0.0)
            for m in range(8):
                if len(found) >= count:
                    break
                block = got[m * nz : (m + 1) * nz, :NT]
                acc = block[0:NG]
                for b in range(1, nzh):
                    acc = acc + block[b * NG : (b + 1) * NG]
                found.append(jnp.concatenate([acc, jnp.zeros((GP - NG, NT), F32)], axis=0))
        return found

    def gather_drain(which):
        wait_rows(z_send_sem.at[which])
        rows = pbuf.at[which, pl.ds(0, np_ - 1)]
        pltpu.make_async_copy(rows, rows, p_send_sem.at[which]).wait()

    zeros = jnp.zeros((PX, CY), F32)
    latitude = ((g * CY + t).astype(F32) + 0.5) / float(CY * NG) - 0.5
    mu10 = 10.0 * jnp.cos(jnp.full((PX, CY), latitude * (math.pi / 2) - 0.4, F32))

    def emission(k):
        square = kel[k] * kel[k]
        return square * square

    def both_passes(k, carry):
        flux_down, flux_up, sun, acc = carry
        em = emission(k)
        trans = jnp.exp(jnp.full((PX, CY), -longwave[k], F32))
        absorbed = 1.0 - trans
        sun_trans = jnp.exp(jnp.full((PX, CY), -shortwave[k], F32))
        raw = absorbed * (flux_down - 2.0 * em) + mu10 * (sun * (1.0 - sun_trans))
        down[k] = raw
        flux_down = trans * flux_down + absorbed * em
        sun = sun * sun_trans
        k2 = LV - 1 - k
        em2 = emission(k2)
        trans2 = jnp.exp(jnp.full((PX, CY), -longwave[k2], F32))
        absorbed2 = 1.0 - trans2
        raw2 = absorbed2 * flux_up
        upw[k2] = raw2
        flux_up = trans2 * flux_up + absorbed2 * em2
        return flux_down, flux_up, sun, acc + (raw + raw2)

    carry = blocked(LV, both_passes, (zeros, emission(LV - 1), jnp.ones((PX, CY), F32), zeros))
    mean = carry[3] * (1.0 / LV)
    for k in range(LV, LP):
        fv[k] = zeros
        smooth1[k] = zeros
        down[k] = zeros
        upw[k] = zeros
        res[k] = zeros
    for ch in range(NCH):
        lv = slice(ch * 16, (ch + 1) * 16)
        heat = down[lv] + upw[lv] - mean[None]
        down[lv] = heat
        hs[:, 0, ch * 128 : (ch + 1) * 128] = heat.reshape(16 * PX, CY).T

    def lines_of(field, dst):
        for ch in range(NCH):
            dst[:, 0, ch * 128 : (ch + 1) * 128] = (
                field[ch * 16 : (ch + 1) * 16].reshape(16 * PX, CY).T
            )

    def columns_of(src, ch):
        top = min(LV, (ch + 1) * 16)
        block = src[:, 0, ch * 128 : (ch + 1) * 128].T.reshape(16, PX, CY)
        return slice(ch * 16, top), block[: top - ch * 16]

    lines_of(fv, fs)

    def factor(k, carry):
        link_above, inv_above = carry
        here = jnp.where(k < LV - 1, link[jnp.minimum(k, LV - 2)], 0.0)
        here = jnp.full((PX, CY), here, F32)
        low = link_above * inv_above
        inv = 1.0 / (4.0 + here + link_above - link_above * low)
        lco[k] = low
        cco[k] = inv
        return here, inv

    blocked(LV, factor, (zeros, zeros))
    lco[LV] = zeros

    def shift_sums(k, carry):
        v = sh[k]
        return carry[0] + v, carry[1] + v * v

    sh_sum, sh_sq = blocked(LV, shift_sums, (zeros, zeros))
    edge_w = row8 == 0
    edge_e = row8 == PX - 1
    edge_s = lane == 0
    edge_n = lane == CY - 1

    def edges(v):
        return [jnp.where(m, v, 0.0) for m in (edge_w, edge_e, edge_s, edge_n)]

    shift_row = pack_row([sh_sum, sh_sq] + edges(sh_sum))

    def column_solve(source, dst):
        def forward(k, above):
            value = source(k) + lco[k] * above
            dst[k] = value
            return value

        blocked(LV, forward, zeros)

        def backward(k, carry):
            below, to_south, to_north = carry
            value = cco[k] * dst[k] + lco[k + 1] * below
            dst[k] = value
            to_south = jnp.where(lane == k, roll(value, k, 1), to_south)
            to_north = jnp.where(lane == k, roll(value, lax.rem(k + 1, CY), 1), to_north)
            return value, to_south, to_north

        return blocked(LV, backward, (zeros, zeros, zeros), reverse=True)

    def halo_copies(n):
        left = (lax.rem(t + NT - 1, NT), g)
        right = (lax.rem(t + 1, NT), g)
        below = (t, lax.rem(g + NG - 1, NG))
        above = (t, lax.rem(g + 1, NG))
        table = (
            (west_send, east_recv, left),
            (east_send, west_recv, right),
            (south_send, north_recv, below),
            (north_send, south_recv, above),
        )
        return [
            pltpu.make_async_remote_copy(
                src_ref=src.at[n],
                dst_ref=dst.at[n],
                send_sem=halo_send_sem.at[n, i],
                recv_sem=halo_recv_sem.at[n, i],
                device_id=device,
                device_id_type=MESH,
            )
            for i, (src, dst, device) in enumerate(table)
        ]

    def halo_fill(n, field, rims):
        west_send[n] = field[0:LV, 0, :]
        east_send[n] = field[0:LV, PX - 1, :]
        south_send[n] = rims[1]
        north_send[n] = rims[2]

    def halo_start(n):
        copies = halo_copies(n)
        for copy in copies:
            copy.start()
        return copies

    def plain_solve(field, dst):
        def forward(k, above):
            value = field[k] + lco[k] * above
            dst[k] = value
            return value

        blocked(LV, forward, zeros)

        def backward(k, below):
            value = cco[k] * dst[k] + lco[k + 1] * below
            dst[k] = value
            return value

        blocked(LV, backward, zeros, reverse=True)

    shift_rims = column_solve(lambda k: sh[k], shift_solve)
    halo_fill(2, shift_solve, shift_rims)

    pl.semaphore_wait(barrier, nz - 1 + np_ - 1 + 2)

    gather_start(0, shift_row)
    turn_start()
    fr[pl.ds(t, 1)] = fs[pl.ds(t, 1)]
    turn_middle()
    halos2 = halo_start(2)
    gather_middle(0)

    mass, m_ss, m_sw, m_se, m_sso, m_sn = gather_end(0, 6)
    grow = iota((GP, NT), 0)
    gcol = iota((GP, NT), 1)
    live_s = ((grow > 0) & (grow < NG)).astype(F32)
    live_n = (grow < NG - 1).astype(F32)
    diagonal = mass + 2.0 * LV * CY + LV * PX * (live_s + live_n)
    couple = float(LV * CY)
    b_co = []
    a_co = []
    for j in range(NG):
        entry = jnp.where(grow == j, diagonal, 0.0)
        near = (grow == j - 1) | (grow == j + 1)
        entry = jnp.where(near & (grow < NG), -float(LV * PX), entry)
        b_co.append(entry)
        a_co.append(jnp.where(grow == j, -couple, 0.0))

    def reduce_step(step, carry):
        hop, a_, b_, c_ = carry
        back = NT - hop
        binv = inverse4(b_)
        alpha = matmul4(a_, [roll(v, hop, 1) for v in binv])
        gamma = matmul4(c_, [roll(v, back, 1) for v in binv])
        alpha = [-v for v in alpha]
        gamma = [-v for v in gamma]
        a_m = [roll(v, hop, 1) for v in a_]
        c_m = [roll(v, hop, 1) for v in c_]
        a_p = [roll(v, back, 1) for v in a_]
        c_p = [roll(v, back, 1) for v in c_]
        ac = matmul4(alpha, c_m)
        ga = matmul4(gamma, a_p)
        b_ = [b_[j] + ac[j] + ga[j] for j in range(NG)]
        a_ = matmul4(alpha, a_m)
        c_ = matmul4(gamma, c_p)
        for j in range(NG):
            alpha_co[step, j] = alpha[j]
            gamma_co[step, j] = gamma[j]
        return hop * 2, tuple(a_), tuple(b_), tuple(c_)

    steps = int(math.log2(NT))
    _, a_f, b_f, c_f = lax.fori_loop(
        0, steps, reduce_step, (jnp.int32(1), tuple(a_co), tuple(b_co), tuple(a_co))
    )
    last = inverse4([a_f[j] + b_f[j] + c_f[j] for j in range(NG)])
    for j in range(NG):
        last_co[j] = last[j]

    def coarse_solve(rhs):
        for step in range(steps):
            hop = 1 << step
            low = roll(rhs, hop, 1)
            high = roll(rhs, NT - hop, 1)
            rhs = (
                rhs
                + matvec4([alpha_co[step, j] for j in range(NG)], low)
                + matvec4([gamma_co[step, j] for j in range(NG)], high)
            )
        return matvec4([last_co[j] for j in range(NG)], rhs)

    def differences(e):
        return (
            e - roll(e, 1, 1),
            e - roll(e, NT - 1, 1),
            live_s * (e - roll(e, 1, 0)),
            live_n * (e - roll(e, GP - 1, 0)),
        )

    mine = (grow == g) & (gcol == t)

    def own(v):
        return total(jnp.where(mine, v, 0.0))

    def rim_of(west, east, south, north):
        return (
            jnp.where(edge_w, west, 0.0)
            + jnp.where(edge_e, east, 0.0)
            + jnp.where(edge_s, south, 0.0)
            + jnp.where(edge_n, north, 0.0)
        )

    long_rim = float(LV * CY)
    short_rim = float(LV * PX)
    corner = float(LV)
    m_shift = (m_sw, m_se, m_sso, m_sn)

    def own_square(e, w):
        cross = (w[0] + w[1]) * (w[2] + w[3])
        value = e * e * m_ss + long_rim * (w[0] * w[0] + w[1] * w[1])
        value = value + short_rim * (w[2] * w[2] + w[3] * w[3]) + 2.0 * corner * cross
        for i in range(4):
            value = value + 2.0 * e * w[i] * m_shift[i]
        return value

    def against(e, w, with_shift, with_edges):
        value = e * with_shift
        for i in range(4):
            value = value + w[i] * with_edges[i]
        return value

    inner_s = edge_s & (g > 0)
    outer_s = edge_s & (g == 0)
    inner_n = edge_n & (g < NG - 1)
    outer_n = edge_n & (g == NG - 1)

    def image_level(v, r, k, west_in, east_in, south_in, north_in):
        west = jnp.where(edge_w, west_in[pl.ds(k, 1), :], roll(v, 1, 0))
        east = jnp.where(edge_e, east_in[pl.ds(k, 1), :], roll(v, PX - 1, 0))
        south = jnp.where(inner_s, roll(south_in, lax.rem(CY - k, CY), 1), roll(v, 1, 1))
        south = jnp.where(outer_s, v, south)
        north = jnp.where(inner_n, roll(north_in, CY - 1 - k, 1), roll(v, CY - 1, 1))
        north = jnp.where(outer_n, v, north)
        return r - ((west + east) + (south + north)) + sh[k] * v

    line_wait((np_ - 1) * nzh, a2a_recv_sem.at[0])
    for ch in range(NCH):
        top = min(LV, (ch + 1) * 16)
        lv = slice(ch * 16, top)
        block = hr[:, :, :, 0, ch * 128 : (ch + 1) * 128].reshape(NT, 128)
        block = block.T.reshape(16, PX, CY)[: top - ch * 16]
        res[lv] = fv[lv] + block

    half = np_ // 2
    rims = column_solve(lambda k: res[k], smooth0)
    halo_fill(0, smooth0, rims)
    halos0 = halo_start(0)
    a2a_start(fs, fr, 1, 0, half)
    for copy in halos0:
        copy.wait_recv()
    south_in = south_recv[0]
    north_in = north_recv[0]

    def moments0(k, carry):
        r_sum, q_sum, rq, rs, qq, qs = carry
        r = res[k]
        q = image_level(
            smooth0[k], r, k, west_recv.at[0], east_recv.at[0], south_in, north_in
        )
        image[k] = q
        s = sh[k]
        return r_sum + r, q_sum + q, rq + r * q, rs + r * s, qq + q * q, qs + q * s

    r_sum, q_sum, rq, rs, qq, qs = blocked(LV, moments0, (zeros,) * 6)
    gather_start(1, pack_row([r_sum - q_sum, rq, rs, qq, qs] + edges(r_sum) + edges(q_sum)))
    image_rims = column_solve(lambda k: image[k], image_solve)
    halo_fill(1, image_solve, image_rims)
    halos1 = halo_start(1)
    a2a_start(fs, fr, 1, half, np_)
    gather_middle(1)
    got = gather_end(1, 13)
    e0 = coarse_solve(got[0])
    w0 = differences(e0)
    m_rq, m_rs, m_qq, m_qs = got[1:5]
    m_re = got[5:9]
    m_qe = got[9:13]
    projection = total(m_rq + against(e0, w0, m_rs, m_re))
    norm0 = total(m_qq + 2.0 * against(e0, w0, m_qs, m_qe) + own_square(e0, w0))
    step0 = projection / norm0
    left_over = projection - step0 * norm0
    i_s = m_qs + against(e0, w0, m_ss, m_shift)
    i_e = (
        m_qe[0] + e0 * m_sw + long_rim * w0[0] + corner * (w0[2] + w0[3]),
        m_qe[1] + e0 * m_se + long_rim * w0[1] + corner * (w0[2] + w0[3]),
        m_qe[2] + e0 * m_sso + short_rim * w0[2] + corner * (w0[0] + w0[1]),
        m_qe[3] + e0 * m_sn + short_rim * w0[3] + corner * (w0[0] + w0[1]),
    )
    at_west = (grow == g) & (gcol == lax.rem(t + NT - 1, NT))
    at_east = (grow == g) & (gcol == lax.rem(t + 1, NT))
    at_south = (grow == g - 1) & (gcol == t)
    at_north = (grow == g + 1) & (gcol == t)
    wanted = [(m, e0) for m in (mine, at_west, at_east, at_south, at_north)]
    wanted = wanted + [(mine, v) for v in w0]
    wanted = wanted + [(at_west, w0[i]) for i in (1, 2, 3)]
    wanted = wanted + [(at_east, w0[i]) for i in (0, 2, 3)]
    wanted = wanted + [(at_south, w0[i]) for i in (3, 0, 1)]
    wanted = wanted + [(at_north, w0[i]) for i in (2, 0, 1)]
    found = [jnp.sum(jnp.where(m, v, 0.0), axis=0, keepdims=True) for m, v in wanted]
    found = found + [jnp.zeros((1, NT), F32)] * (24 - len(found))
    found = jnp.sum(jnp.concatenate(found, axis=0), axis=1, keepdims=True)
    found = [found[i : i + 1] for i in range(21)]
    e0_own, e_west, e_east, e_south, e_north = found[0:5]
    rim0 = rim_of(*found[5:9])
    lane1 = iota((1, CY), 1)
    row1 = iota((PX, 1), 0)

    def rim_row(f):
        return f[0] + jnp.where(lane1 == 0, f[1], 0.0) + jnp.where(lane1 == CY - 1, f[2], 0.0)

    def rim_col(f):
        return f[0] + jnp.where(row1 == 0, f[1], 0.0) + jnp.where(row1 == PX - 1, f[2], 0.0)

    for copy in halos2 + halos1:
        copy.wait_recv()

    def ghost(recv, e, rim):
        return recv[0] - step0 * (recv[1] + e * recv[2] + 0.25 * rim)

    ghost_west[...] = ghost(west_recv, e_west, rim_row(found[9:12]))
    ghost_east[...] = ghost(east_recv, e_east, rim_row(found[12:15]))
    ghost_south = ghost(south_recv, e_south, rim_col(found[15:18]))
    ghost_north = ghost(north_recv, e_north, rim_col(found[18:21]))

    quarter_rim = 0.25 * rim0

    def moments1(k, carry):
        r_sum, q_sum, rq, rs, qq, qs, iq = carry
        s = sh[k]
        q0 = image[k] + s * e0_own + rim0
        r = res[k] - step0 * q0
        v = smooth0[k] - step0 * (image_solve[k] + e0_own * shift_solve[k] + quarter_rim)
        smooth1[k] = v
        q = image_level(v, r, k, ghost_west, ghost_east, ghost_south, ghost_north)
        return (
            r_sum + r,
            q_sum + q,
            rq + r * q,
            rs + r * s,
            qq + q * q,
            qs + q * s,
            iq + q0 * q,
        )

    r_sum, q_sum, rq, rs, qq, qs, iq = blocked(LV, moments1, (zeros,) * 7)
    gather_start(2, pack_row([r_sum - q_sum, rq, rs, qq, qs] + edges(r_sum) + edges(q_sum) + [iq]))
    lines_of(smooth1, xs)
    a2a_start(xs, xr, 2, 0, half)
    xr[pl.ds(t, 1)] = xs[pl.ds(t, 1)]

    a2a_wait(1)
    for ch in range(NCH):
        lv, block = columns_of(fr, ch)
        down[lv] = down[lv] + block
    plain_solve(down, upw)

    gather_middle(2)
    a2a_start(xs, xr, 2, half, np_)
    got = gather_end(2, 14)
    e1 = coarse_solve(got[0])
    w1 = differences(e1)
    m_rq, m_rs, m_qq, m_qs = got[1:5]
    m_re = got[5:9]
    m_qe = got[9:13]
    crossing = total(got[13] + against(e1, w1, i_s, i_e))
    projection1 = total(m_rq + against(e1, w1, m_rs, m_re))
    square1 = total(m_qq + 2.0 * against(e1, w1, m_qs, m_qe) + own_square(e1, w1))
    weight = crossing / norm0
    norm1 = square1 - weight * crossing
    step1 = (projection1 - weight * left_over) / norm1
    scale0 = step0 - step1 * weight
    block_part = scale0 * e0 + step1 * e1
    constant = own(block_part)
    by_tile = jnp.sum(jnp.where(grow == g, block_part, 0.0), axis=0, keepdims=True)

    def finish(k, _):
        out_field[k] = scale0 * smooth0[k] + step1 * smooth1[k] + constant
        return 0

    blocked(LV, finish, 0)

    a2a_wait(2)
    for ch in range(NCH):
        lv, block = columns_of(xr, ch)
        out_rad[lv] = scale0 * upw[lv] + step1 * block + by_tile[None]

    line_wait((np_ - 1) * nzh, a2a_send_sem.at[0])
    line_wait((nzh - 1) * np_, turn_send_sem)
    for which in range(3):
        if which > 0:
            a2a_drain(which)
        gather_drain(which)
    for copy in halos0 + halos1 + halos2:
        copy.wait_send()


def per_device(fv, sh, link, kel, longwave, shortwave):
    vmem = pl.BlockSpec(memory_space=pltpu.VMEM)
    hbm = pl.BlockSpec(memory_space=pltpu.HBM)
    field = jax.ShapeDtypeStruct((LV, PX, CY), F32)
    np_ = DIMS[0] * DIMS[2] * DIMS[3]
    steps = int(math.log2(NT))
    padded = pltpu.VMEM((LP, PX, CY), F32)
    whole = pltpu.VMEM((LV, PX, CY), F32)
    lines = pltpu.VMEM((NT, 1, LP * PX), F32)
    middle = pltpu.VMEM((DIMS[1], np_, 1, LP * PX), F32)
    turned = pltpu.VMEM((DIMS[0], DIMS[1], DIMS[2] * DIMS[3], 1, LP * PX), F32)
    rims = pltpu.VMEM((3, LV, CY), F32)
    corners = pltpu.VMEM((3, PX, CY), F32)
    dma = pltpu.SemaphoreType.DMA
    return pl.pallas_call(
        kernel,
        out_shape=(field, field),
        in_specs=[hbm] * 6,
        out_specs=(vmem, vmem),
        scratch_shapes=[padded, whole, whole]
        + [pltpu.SMEM((LV - 1,), F32), pltpu.SMEM((LV,), F32), pltpu.SMEM((LV,), F32)]
        + [padded] * 10
        + [lines, middle, turned]
        + [lines] * 4
        + [rims, rims, corners, corners, rims, rims, corners, corners]
        + [
            pltpu.VMEM((3, DIMS[1] * NG, 128), F32),
            pltpu.VMEM((3, np_, NM // 8, 128), F32),
            pltpu.VMEM((steps, NG, GP, NT), F32),
            pltpu.VMEM((steps, NG, GP, NT), F32),
            pltpu.VMEM((NG, GP, NT), F32),
            pltpu.VMEM((NT - 1, 1, LP * PX), F32),
            pltpu.VMEM((DIMS[1] * NG, 1, 128), F32),
            pltpu.VMEM((LV, CY), F32),
            pltpu.VMEM((LV, CY), F32),
            dma,
            dma((DIMS[0],)),
            dma((DIMS[0],)),
            dma,
            dma((6,)),
            dma((3,)),
            dma((3,)),
            dma((3, 4)),
            dma((3, 4)),
            dma((3,)),
            dma((3,)),
            dma((3,)),
            dma((3,)),
        ],
        compiler_params=pltpu.CompilerParams(
            collective_id=0, has_side_effects=True, vmem_limit_bytes=67043328
        ),
        name="step",
    )(fv, sh, kel, link, longwave, shortwave)


def solution(mesh):
    spread = P(None, "tile", "grp")
    columns = P(None, None, ("tile", "grp"))
    return jax.shard_map(
        per_device,
        mesh=mesh,
        in_specs=(spread, spread, P(), columns, P(), P()),
        out_specs=(spread, columns),
        check_vma=False,
    )
```

```python
import math

import jax
import jax.numpy as jnp
from jax import lax
from jax.experimental import pallas as pl
from jax.experimental.pallas import tpu as pltpu
from jax.sharding import PartitionSpec as P

LV = 70
PX = 8
CY = 128
NG = 4
DIMS = (4, 4, 4, 2)
NT = 128
LP = 80
NCH = LP // 16
UNROLL = 10
NM = 16
GP = 8
F32 = jnp.float32
MESH = pl.DeviceIdType.MESH


def iota(shape, dim):
    return lax.broadcasted_iota(jnp.int32, shape, dim)


def roll(value, shift, axis):
    return pltpu.roll(value, shift, axis)


def blocked(levels, body, init, reverse=False):
    def trip(b, carry):
        for j in range(UNROLL):
            k = b * UNROLL + j
            carry = body(levels - 1 - k if reverse else k, carry)
        return carry

    return lax.fori_loop(0, levels // UNROLL, trip, init)


def total(value):
    return jnp.sum(jnp.sum(value, axis=0, keepdims=True), axis=1, keepdims=True)


def matmul4(left, right):
    out = []
    for j in range(NG):
        term = left[0] * right[j][0:1, :]
        for l in range(1, NG):
            term = term + left[l] * right[j][l : l + 1, :]
        out.append(term)
    return out


def inverse4(columns):
    columns = list(columns)
    row = iota((GP, NT), 0)
    for k in range(NG):
        pivot = 1.0 / columns[k][k : k + 1, :]
        for j in range(NG):
            if j != k:
                scaled = columns[j][k : k + 1, :] * pivot
                columns[j] = jnp.where(row == k, scaled, columns[j] - columns[k] * scaled)
        columns[k] = jnp.where(row == k, pivot, -columns[k] * pivot)
    return columns


def matvec4(columns, vector):
    out = columns[0] * vector[0:1, :]
    for l in range(1, NG):
        out = out + columns[l] * vector[l : l + 1, :]
    return out


def kernel(
    fv_hbm,
    sh_hbm,
    kel_hbm,
    link_hbm,
    longwave_hbm,
    shortwave_hbm,
    out_field,
    out_rad,
    fv,
    sh,
    kel,
    link,
    longwave,
    shortwave,
    down,
    upw,
    lco,
    cco,
    res,
    smooth0,
    smooth1,
    image,
    shift_solve,
    image_solve,
    hs,
    mid,
    hr,
    fs,
    fr,
    xs,
    xr,
    west_send,
    east_send,
    south_send,
    north_send,
    west_recv,
    east_recv,
    south_recv,
    north_recv,
    zbuf,
    pbuf,
    alpha_co,
    gamma_co,
    last_co,
    line_count,
    row_count,
    ghost_west,
    ghost_east,
    turn_send_sem,
    turn_recv_sem,
    turn_own_sem,
    own_sem,
    in_sem,
    a2a_send_sem,
    a2a_recv_sem,
    halo_send_sem,
    halo_recv_sem,
    z_send_sem,
    z_recv_sem,
    p_send_sem,
    p_recv_sem,
):
    ny, nzh, nx, nc = DIMS
    nz = nzh * NG
    np_ = ny * nx * nc
    t = lax.axis_index("tile")
    g = lax.axis_index("grp")
    c = lax.rem(t, nc)
    x = lax.rem(lax.div(t, nc), nx)
    zh = lax.rem(lax.div(t, nc * nx), nzh)
    y = lax.div(t, nc * nx * nzh)
    z = zh * NG + g
    p = (y * nx + x) * nc + c

    def tile_of(y_, zh_, x_, c_):
        return ((y_ * nzh + zh_) * nx + x_) * nc + c_

    z_part = [lax.rem(zh + dz, nzh) * (nx * nc) for dz in range(nzh)]
    z_order = sorted(range(nzh), key=lambda dz: -min(dz, nzh - dz))

    def plane_base(r):
        dc = lax.rem(r, nc)
        dx = lax.rem(lax.div(r, nc), nx)
        dy = lax.div(r, nc * nx)
        low = lax.rem(x + dx, nx) * nc + lax.rem(c + dc, nc)
        return lax.rem(y + dy, ny) * (nzh * nx * nc) + low

    def each_tile(low, high, act):
        if low == 0:
            base = plane_base(0)
            for dz in z_order[:-1]:
                act(base + z_part[dz])

        def some(r, _):
            base = plane_base(r)
            for dz in z_order:
                act(base + z_part[dz])
            return 0

        lax.fori_loop(max(low, 1), high, some, 0)

    def each_plane(act):
        def one(r, _):
            act(r)
            return 0

        lax.fori_loop(1, np_, one, 0)

    plane_here = plane_base(0)

    def each_z(first, act):
        if first == 0:
            for dz in z_order[:-1]:
                act(plane_here + z_part[dz], g)

        def some(dg, _):
            g2 = lax.rem(g + dg, NG)
            for dz in z_order:
                act(plane_here + z_part[dz], g2)
            return 0

        lax.fori_loop(1, NG, some, 0)

    barrier = pltpu.get_barrier_semaphore()

    def greet(tile, grp):
        pl.semaphore_signal(barrier, inc=1, device_id=(tile, grp), device_id_type=MESH)

    ring_before = lax.rem(t + NT - 1, NT)
    ring_after = lax.rem(t + 1, NT)
    each_z(0, greet)
    each_plane(lambda r: greet(plane_base(r) + z_part[0], g))
    greet(ring_before, g)
    greet(ring_after, g)
    pairs = (
        (kel_hbm, kel),
        (longwave_hbm, longwave),
        (shortwave_hbm, shortwave),
        (link_hbm, link),
        (sh_hbm, sh),
        (fv_hbm, fv.at[pl.ds(0, LV)]),
    )
    loads = [pltpu.make_async_copy(src, dst, in_sem.at[i]) for i, (src, dst) in enumerate(pairs)]
    for load in loads:
        load.start()
    for load in loads:
        load.wait()

    def wait_lines(sem):
        pltpu.make_async_copy(line_count, line_count, sem).wait()

    def wait_rows(sem):
        rows = row_count.at[pl.ds(0, nz - 1)]
        pltpu.make_async_copy(rows, rows, sem).wait()

    def a2a_start(src, dst, which, low, high):
        def send(peer):
            pltpu.make_async_remote_copy(
                src_ref=src.at[pl.ds(peer, 1)],
                dst_ref=dst.at[pl.ds(t, 1)],
                send_sem=a2a_send_sem.at[which],
                recv_sem=a2a_recv_sem.at[which],
                device_id=(peer, g),
                device_id_type=MESH,
            ).start()

        each_tile(low, high, send)

    nxc = nx * nc
    xc = lax.rem(t, nxc)

    def turn_rows(dy):
        return lax.rem(y + dy, ny)

    def turn_start():
        for dy in range(ny):
            y2 = turn_rows(dy)
            for dz in z_order[:-1]:
                peer = plane_here + z_part[dz]
                zh2 = lax.rem(zh + dz, nzh)
                pltpu.make_async_remote_copy(
                    src_ref=hs.at[pl.ds((y2 * nzh + zh2) * nxc, nxc)],
                    dst_ref=mid.at[zh, pl.ds(y2 * nxc, nxc)],
                    send_sem=turn_send_sem,
                    recv_sem=turn_recv_sem.at[dy],
                    device_id=(peer, g),
                    device_id_type=MESH,
                ).start()
            pltpu.make_async_copy(
                hs.at[pl.ds((y2 * nzh + zh) * nxc, nxc)],
                mid.at[zh, pl.ds(y2 * nxc, nxc)],
                turn_own_sem.at[dy],
            ).start()

    def line_wait(count, sem):
        part = line_count.at[pl.ds(0, count)]
        pltpu.make_async_copy(part, part, sem).wait()

    def turn_middle():
        for dy in range(ny):
            y2 = turn_rows(dy)
            line_wait((nzh - 1) * nxc, turn_recv_sem.at[dy])
            line_wait(nxc, turn_own_sem.at[dy])

            def one(r, _, y2=y2):
                xc2 = lax.rem(xc + r, nxc)
                pltpu.make_async_remote_copy(
                    src_ref=mid.at[:, y2 * nxc + xc2],
                    dst_ref=hr.at[y, :, xc],
                    send_sem=a2a_send_sem.at[0],
                    recv_sem=a2a_recv_sem.at[0],
                    device_id=((y2 * nzh + zh) * nxc + xc2, g),
                    device_id_type=MESH,
                ).start()
                return 0

            lax.fori_loop(1 if dy == 0 else 0, nxc, one, 0)
        own_copy = pltpu.make_async_copy(mid.at[:, p], hr.at[y, :, xc], own_sem)
        own_copy.start()
        own_copy.wait()

    def a2a_wait(which):
        wait_lines(a2a_recv_sem.at[which])

    def a2a_drain(which):
        wait_lines(a2a_send_sem.at[which])

    lane = iota((PX, CY), 1)
    row8 = iota((PX, CY), 0)

    def pack_row(values):
        rows = [jnp.sum(v, axis=0, keepdims=True) for v in values]
        rows = rows + [jnp.zeros((1, CY), F32)] * (NM - len(rows))
        sums = jnp.sum(jnp.concatenate(rows, axis=0), axis=1, keepdims=True)
        diag = iota((NM, 128), 0) == iota((NM, 128), 1)
        return jnp.sum(jnp.where(diag, sums, 0.0), axis=0, keepdims=True)

    def gather_start(which, row):
        buf = zbuf.at[which]
        buf[pl.ds(z, 1), :] = row

        def send(tile, grp):
            pltpu.make_async_remote_copy(
                src_ref=buf.at[pl.ds(z, 1), :],
                dst_ref=buf.at[pl.ds(z, 1), :],
                send_sem=z_send_sem.at[which],
                recv_sem=z_recv_sem.at[which],
                device_id=(tile, grp),
                device_id_type=MESH,
            ).start()

        each_z(0, send)

    def gather_middle(which):
        buf = zbuf.at[which]
        wait_rows(z_recv_sem.at[which])
        value = buf[...]
        ln = iota((nz, 128), 1)
        mine = lax.rem(ln, nz) == iota((nz, 128), 0)
        packed = []
        for r in range(NM // 8):
            spread = jnp.take_along_axis(value, lax.rem(r * 8 + lax.div(ln, nz), 128), axis=1)
            packed.append(jnp.sum(jnp.where(mine, spread, 0.0), axis=0, keepdims=True))
        pbuf[which, pl.ds(p, 1)] = jnp.concatenate(packed, axis=0)[None]
        dst = pbuf.at[which]

        def send(r, _):
            pltpu.make_async_remote_copy(
                src_ref=dst.at[pl.ds(p, 1)],
                dst_ref=dst.at[pl.ds(p, 1)],
                send_sem=p_send_sem.at[which],
                recv_sem=p_recv_sem.at[which],
                device_id=(plane_base(r) + z_part[0], g),
                device_id_type=MESH,
            ).start()
            return 0

        lax.fori_loop(1, np_, send, 0)

    def gather_end(which, count):
        rows = pbuf.at[which, pl.ds(0, np_ - 1)]
        pltpu.make_async_copy(rows, rows, p_recv_sem.at[which]).wait()
        parts = [pbuf[which, :, r, :] for r in range(NM // 8)]
        parts.append(jnp.zeros((128 - np_ * (NM // 8), 128), F32))
        flat = jnp.concatenate(parts, axis=0).T
        ln = iota((128, 128), 1)
        rw = iota((128, 128), 0)
        t_p = (lax.rem(lax.div(ln, nc * nx * nzh), ny) * nx * nc) + lax.rem(ln, nx * nc)
        t_zh = lax.rem(lax.div(ln, nc * nx), nzh)
        keep = lax.div(lax.rem(rw, nz), NG) == t_zh
        found = []
        for r in range(NM // 8):
            if len(found) >= count:
                break
            got = jnp.take_along_axis(flat, t_p + r * np_, axis=1)
            got = jnp.where(keep, got, 0.0)
            for m in range(8):
                if len(found) >= count:
                    break
                block = got[m * nz : (m + 1) * nz, :NT]
                acc = block[0:NG]
                for b in range(1, nzh):
                    acc = acc + block[b * NG : (b + 1) * NG]
                found.append(jnp.concatenate([acc, jnp.zeros((GP - NG, NT), F32)], axis=0))
        return found

    def gather_drain(which):
        wait_rows(z_send_sem.at[which])
        rows = pbuf.at[which, pl.ds(0, np_ - 1)]
        pltpu.make_async_copy(rows, rows, p_send_sem.at[which]).wait()

    zeros = jnp.zeros((PX, CY), F32)
    latitude = ((g * CY + t).astype(F32) + 0.5) / float(CY * NG) - 0.5
    mu10 = 10.0 * jnp.cos(jnp.full((PX, CY), latitude * (math.pi / 2) - 0.4, F32))

    def emission(k):
        square = kel[k] * kel[k]
        return square * square

    def both_passes(k, carry):
        flux_down, flux_up, sun, acc = carry
        em = emission(k)
        trans = jnp.exp(jnp.full((PX, CY), -longwave[k], F32))
        absorbed = 1.0 - trans
        sun_trans = jnp.exp(jnp.full((PX, CY), -shortwave[k], F32))
        raw = absorbed * (flux_down - 2.0 * em) + mu10 * (sun * (1.0 - sun_trans))
        down[k] = raw
        flux_down = trans * flux_down + absorbed * em
        sun = sun * sun_trans
        k2 = LV - 1 - k
        em2 = emission(k2)
        trans2 = jnp.exp(jnp.full((PX, CY), -longwave[k2], F32))
        absorbed2 = 1.0 - trans2
        raw2 = absorbed2 * flux_up
        upw[k2] = raw2
        flux_up = trans2 * flux_up + absorbed2 * em2
        return flux_down, flux_up, sun, acc + (raw + raw2)

    carry = blocked(LV, both_passes, (zeros, emission(LV - 1), jnp.ones((PX, CY), F32), zeros))
    mean = carry[3] * (1.0 / LV)
    for k in range(LV, LP):
        fv[k] = zeros
        smooth1[k] = zeros
        down[k] = zeros
        upw[k] = zeros
        res[k] = zeros
    for ch in range(NCH):
        lv = slice(ch * 16, (ch + 1) * 16)
        heat = down[lv] + upw[lv] - mean[None]
        down[lv] = heat
        hs[:, 0, ch * 128 : (ch + 1) * 128] = heat.reshape(16 * PX, CY).T

    def lines_of(field, dst):
        for ch in range(NCH):
            dst[:, 0, ch * 128 : (ch + 1) * 128] = (
                field[ch * 16 : (ch + 1) * 16].reshape(16 * PX, CY).T
            )

    def columns_of(src, ch):
        top = min(LV, (ch + 1) * 16)
        block = src[:, 0, ch * 128 : (ch + 1) * 128].T.reshape(16, PX, CY)
        return slice(ch * 16, top), block[: top - ch * 16]

    lines_of(fv, fs)

    def factor(k, carry):
        link_above, inv_above = carry
        here = jnp.where(k < LV - 1, link[jnp.minimum(k, LV - 2)], 0.0)
        here = jnp.full((PX, CY), here, F32)
        low = link_above * inv_above
        inv = 1.0 / (4.0 + here + link_above - link_above * low)
        lco[k] = low
        cco[k] = inv
        return here, inv

    blocked(LV, factor, (zeros, zeros))
    lco[LV] = zeros

    def shift_sums(k, carry):
        v = sh[k]
        return carry[0] + v, carry[1] + v * v

    sh_sum, sh_sq = blocked(LV, shift_sums, (zeros, zeros))
    edge_w = row8 == 0
    edge_e = row8 == PX - 1
    edge_s = lane == 0
    edge_n = lane == CY - 1

    def edges(v):
        return [jnp.where(m, v, 0.0) for m in (edge_w, edge_e, edge_s, edge_n)]

    shift_row = pack_row([sh_sum, sh_sq] + edges(sh_sum))

    def column_solve(source, dst):
        def forward(k, above):
            value = source(k) + lco[k] * above
            dst[k] = value
            return value

        blocked(LV, forward, zeros)

        def backward(k, carry):
            below, to_south, to_north = carry
            value = cco[k] * dst[k] + lco[k + 1] * below
            dst[k] = value
            to_south = jnp.where(lane == k, roll(value, k, 1), to_south)
            to_north = jnp.where(lane == k, roll(value, lax.rem(k + 1, CY), 1), to_north)
            return value, to_south, to_north

        return blocked(LV, backward, (zeros, zeros, zeros), reverse=True)

    def halo_copies(n):
        left = (lax.rem(t + NT - 1, NT), g)
        right = (lax.rem(t + 1, NT), g)
        below = (t, lax.rem(g + NG - 1, NG))
        above = (t, lax.rem(g + 1, NG))
        table = (
            (west_send, east_recv, left),
            (east_send, west_recv, right),
            (south_send, north_recv, below),
            (north_send, south_recv, above),
        )
        return [
            pltpu.make_async_remote_copy(
                src_ref=src.at[n],
                dst_ref=dst.at[n],
                send_sem=halo_send_sem.at[n, i],
                recv_sem=halo_recv_sem.at[n, i],
                device_id=device,
                device_id_type=MESH,
            )
            for i, (src, dst, device) in enumerate(table)
        ]

    def halo_fill(n, field, rims):
        west_send[n] = field[0:LV, 0, :]
        east_send[n] = field[0:LV, PX - 1, :]
        south_send[n] = rims[1]
        north_send[n] = rims[2]

    def halo_start(n):
        copies = halo_copies(n)
        for copy in copies:
            copy.start()
        return copies

    def plain_solve(field, dst):
        def forward(k, above):
            value = field[k] + lco[k] * above
            dst[k] = value
            return value

        blocked(LV, forward, zeros)

        def backward(k, below):
            value = cco[k] * dst[k] + lco[k + 1] * below
            dst[k] = value
            return value

        blocked(LV, backward, zeros, reverse=True)

    shift_rims = column_solve(lambda k: sh[k], shift_solve)
    halo_fill(2, shift_solve, shift_rims)

    pl.semaphore_wait(barrier, nz - 1 + np_ - 1 + 2)

    gather_start(0, shift_row)
    turn_start()
    fr[pl.ds(t, 1)] = fs[pl.ds(t, 1)]
    turn_middle()
    halos2 = halo_start(2)
    gather_middle(0)

    mass, m_ss, m_sw, m_se, m_sso, m_sn = gather_end(0, 6)
    grow = iota((GP, NT), 0)
    gcol = iota((GP, NT), 1)
    live_s = ((grow > 0) & (grow < NG)).astype(F32)
    live_n = (grow < NG - 1).astype(F32)
    diagonal = mass + 2.0 * LV * CY + LV * PX * (live_s + live_n)
    couple = float(LV * CY)
    b_co = []
    a_co = []
    for j in range(NG):
        entry = jnp.where(grow == j, diagonal, 0.0)
        near = (grow == j - 1) | (grow == j + 1)
        entry = jnp.where(near & (grow < NG), -float(LV * PX), entry)
        b_co.append(entry)
        a_co.append(jnp.where(grow == j, -couple, 0.0))

    def reduce_step(step, carry):
        hop, a_, b_, c_ = carry
        back = NT - hop
        binv = inverse4(b_)
        alpha = matmul4(a_, [roll(v, hop, 1) for v in binv])
        gamma = matmul4(c_, [roll(v, back, 1) for v in binv])
        alpha = [-v for v in alpha]
        gamma = [-v for v in gamma]
        a_m = [roll(v, hop, 1) for v in a_]
        c_m = [roll(v, hop, 1) for v in c_]
        a_p = [roll(v, back, 1) for v in a_]
        c_p = [roll(v, back, 1) for v in c_]
        ac = matmul4(alpha, c_m)
        ga = matmul4(gamma, a_p)
        b_ = [b_[j] + ac[j] + ga[j] for j in range(NG)]
        a_ = matmul4(alpha, a_m)
        c_ = matmul4(gamma, c_p)
        for j in range(NG):
            alpha_co[step, j] = alpha[j]
            gamma_co[step, j] = gamma[j]
        return hop * 2, tuple(a_), tuple(b_), tuple(c_)

    steps = int(math.log2(NT))
    _, a_f, b_f, c_f = lax.fori_loop(
        0, steps, reduce_step, (jnp.int32(1), tuple(a_co), tuple(b_co), tuple(a_co))
    )
    last = inverse4([a_f[j] + b_f[j] + c_f[j] for j in range(NG)])
    for j in range(NG):
        last_co[j] = last[j]

    def coarse_solve(rhs):
        for step in range(steps):
            hop = 1 << step
            low = roll(rhs, hop, 1)
            high = roll(rhs, NT - hop, 1)
            rhs = (
                rhs
                + matvec4([alpha_co[step, j] for j in range(NG)], low)
                + matvec4([gamma_co[step, j] for j in range(NG)], high)
            )
        return matvec4([last_co[j] for j in range(NG)], rhs)

    def differences(e):
        return (
            e - roll(e, 1, 1),
            e - roll(e, NT - 1, 1),
            live_s * (e - roll(e, 1, 0)),
            live_n * (e - roll(e, GP - 1, 0)),
        )

    mine = (grow == g) & (gcol == t)

    def own(v):
        return total(jnp.where(mine, v, 0.0))

    def rim_of(west, east, south, north):
        return (
            jnp.where(edge_w, west, 0.0)
            + jnp.where(edge_e, east, 0.0)
            + jnp.where(edge_s, south, 0.0)
            + jnp.where(edge_n, north, 0.0)
        )

    long_rim = float(LV * CY)
    short_rim = float(LV * PX)
    corner = float(LV)
    m_shift = (m_sw, m_se, m_sso, m_sn)

    def own_square(e, w):
        cross = (w[0] + w[1]) * (w[2] + w[3])
        value = e * e * m_ss + long_rim * (w[0] * w[0] + w[1] * w[1])
        value = value + short_rim * (w[2] * w[2] + w[3] * w[3]) + 2.0 * corner * cross
        for i in range(4):
            value = value + 2.0 * e * w[i] * m_shift[i]
        return value

    def against(e, w, with_shift, with_edges):
        value = e * with_shift
        for i in range(4):
            value = value + w[i] * with_edges[i]
        return value

    inner_s = edge_s & (g > 0)
    outer_s = edge_s & (g == 0)
    inner_n = edge_n & (g < NG - 1)
    outer_n = edge_n & (g == NG - 1)

    def image_level(v, r, k, west_in, east_in, south_in, north_in):
        west = jnp.where(edge_w, west_in[pl.ds(k, 1), :], roll(v, 1, 0))
        east = jnp.where(edge_e, east_in[pl.ds(k, 1), :], roll(v, PX - 1, 0))
        south = jnp.where(inner_s, roll(south_in, lax.rem(CY - k, CY), 1), roll(v, 1, 1))
        south = jnp.where(outer_s, v, south)
        north = jnp.where(inner_n, roll(north_in, CY - 1 - k, 1), roll(v, CY - 1, 1))
        north = jnp.where(outer_n, v, north)
        return r - ((west + east) + (south + north)) + sh[k] * v

    line_wait((np_ - 1) * nzh, a2a_recv_sem.at[0])
    for ch in range(NCH):
        top = min(LV, (ch + 1) * 16)
        lv = slice(ch * 16, top)
        block = hr[:, :, :, 0, ch * 128 : (ch + 1) * 128].reshape(NT, 128)
        block = block.T.reshape(16, PX, CY)[: top - ch * 16]
        res[lv] = fv[lv] + block

    half = np_ // 2
    rims = column_solve(lambda k: res[k], smooth0)
    halo_fill(0, smooth0, rims)
    halos0 = halo_start(0)
    a2a_start(fs, fr, 1, 0, half)
    for copy in halos0:
        copy.wait_recv()
    south_in = south_recv[0]
    north_in = north_recv[0]

    def moments0(k, carry):
        r_sum, q_sum, rq, rs, qq, qs = carry
        r = res[k]
        q = image_level(
            smooth0[k], r, k, west_recv.at[0], east_recv.at[0], south_in, north_in
        )
        image[k] = q
        s = sh[k]
        return r_sum + r, q_sum + q, rq + r * q, rs + r * s, qq + q * q, qs + q * s

    r_sum, q_sum, rq, rs, qq, qs = blocked(LV, moments0, (zeros,) * 6)
    gather_start(1, pack_row([r_sum - q_sum, rq, rs, qq, qs] + edges(r_sum) + edges(q_sum)))
    image_rims = column_solve(lambda k: image[k], image_solve)
    halo_fill(1, image_solve, image_rims)
    halos1 = halo_start(1)
    a2a_start(fs, fr, 1, half, np_)
    gather_middle(1)
    got = gather_end(1, 13)
    e0 = coarse_solve(got[0])
    w0 = differences(e0)
    m_rq, m_rs, m_qq, m_qs = got[1:5]
    m_re = got[5:9]
    m_qe = got[9:13]
    projection = total(m_rq + against(e0, w0, m_rs, m_re))
    norm0 = total(m_qq + 2.0 * against(e0, w0, m_qs, m_qe) + own_square(e0, w0))
    step0 = projection / norm0
    left_over = projection - step0 * norm0
    i_s = m_qs + against(e0, w0, m_ss, m_shift)
    i_e = (
        m_qe[0] + e0 * m_sw + long_rim * w0[0] + corner * (w0[2] + w0[3]),
        m_qe[1] + e0 * m_se + long_rim * w0[1] + corner * (w0[2] + w0[3]),
        m_qe[2] + e0 * m_sso + short_rim * w0[2] + corner * (w0[0] + w0[1]),
        m_qe[3] + e0 * m_sn + short_rim * w0[3] + corner * (w0[0] + w0[1]),
    )
    at_west = (grow == g) & (gcol == lax.rem(t + NT - 1, NT))
    at_east = (grow == g) & (gcol == lax.rem(t + 1, NT))
    at_south = (grow == g - 1) & (gcol == t)
    at_north = (grow == g + 1) & (gcol == t)
    wanted = [(m, e0) for m in (mine, at_west, at_east, at_south, at_north)]
    wanted = wanted + [(mine, v) for v in w0]
    wanted = wanted + [(at_west, w0[i]) for i in (1, 2, 3)]
    wanted = wanted + [(at_east, w0[i]) for i in (0, 2, 3)]
    wanted = wanted + [(at_south, w0[i]) for i in (3, 0, 1)]
    wanted = wanted + [(at_north, w0[i]) for i in (2, 0, 1)]
    found = [jnp.sum(jnp.where(m, v, 0.0), axis=0, keepdims=True) for m, v in wanted]
    found = found + [jnp.zeros((1, NT), F32)] * (24 - len(found))
    found = jnp.sum(jnp.concatenate(found, axis=0), axis=1, keepdims=True)
    found = [found[i : i + 1] for i in range(21)]
    e0_own, e_west, e_east, e_south, e_north = found[0:5]
    rim0 = rim_of(*found[5:9])
    lane1 = iota((1, CY), 1)
    row1 = iota((PX, 1), 0)

    def rim_row(f):
        return f[0] + jnp.where(lane1 == 0, f[1], 0.0) + jnp.where(lane1 == CY - 1, f[2], 0.0)

    def rim_col(f):
        return f[0] + jnp.where(row1 == 0, f[1], 0.0) + jnp.where(row1 == PX - 1, f[2], 0.0)

    for copy in halos2 + halos1:
        copy.wait_recv()

    def ghost(recv, e, rim):
        return recv[0] - step0 * (recv[1] + e * recv[2] + 0.25 * rim)

    ghost_west[...] = ghost(west_recv, e_west, rim_row(found[9:12]))
    ghost_east[...] = ghost(east_recv, e_east, rim_row(found[12:15]))
    ghost_south = ghost(south_recv, e_south, rim_col(found[15:18]))
    ghost_north = ghost(north_recv, e_north, rim_col(found[18:21]))

    quarter_rim = 0.25 * rim0

    def moments1(k, carry):
        r_sum, q_sum, rq, rs, qq, qs, iq = carry
        s = sh[k]
        q0 = image[k] + s * e0_own + rim0
        r = res[k] - step0 * q0
        v = smooth0[k] - step0 * (image_solve[k] + e0_own * shift_solve[k] + quarter_rim)
        smooth1[k] = v
        q = image_level(v, r, k, ghost_west, ghost_east, ghost_south, ghost_north)
        return (
            r_sum + r,
            q_sum + q,
            rq + r * q,
            rs + r * s,
            qq + q * q,
            qs + q * s,
            iq + q0 * q,
        )

    r_sum, q_sum, rq, rs, qq, qs, iq = blocked(LV, moments1, (zeros,) * 7)
    gather_start(2, pack_row([r_sum - q_sum, rq, rs, qq, qs] + edges(r_sum) + edges(q_sum) + [iq]))
    lines_of(smooth1, xs)
    a2a_start(xs, xr, 2, 0, np_)
    xr[pl.ds(t, 1)] = xs[pl.ds(t, 1)]

    gather_middle(2)
    a2a_wait(1)
    for ch in range(NCH):
        lv, block = columns_of(fr, ch)
        down[lv] = down[lv] + block
    plain_solve(down, upw)

    got = gather_end(2, 14)
    e1 = coarse_solve(got[0])
    w1 = differences(e1)
    m_rq, m_rs, m_qq, m_qs = got[1:5]
    m_re = got[5:9]
    m_qe = got[9:13]
    crossing = total(got[13] + against(e1, w1, i_s, i_e))
    projection1 = total(m_rq + against(e1, w1, m_rs, m_re))
    square1 = total(m_qq + 2.0 * against(e1, w1, m_qs, m_qe) + own_square(e1, w1))
    weight = crossing / norm0
    norm1 = square1 - weight * crossing
    step1 = (projection1 - weight * left_over) / norm1
    scale0 = step0 - step1 * weight
    block_part = scale0 * e0 + step1 * e1
    constant = own(block_part)
    by_tile = jnp.sum(jnp.where(grow == g, block_part, 0.0), axis=0, keepdims=True)

    def finish(k, _):
        out_field[k] = scale0 * smooth0[k] + step1 * smooth1[k] + constant
        return 0

    blocked(LV, finish, 0)

    a2a_wait(2)
    for ch in range(NCH):
        lv, block = columns_of(xr, ch)
        out_rad[lv] = scale0 * upw[lv] + step1 * block + by_tile[None]

    line_wait((np_ - 1) * nzh, a2a_send_sem.at[0])
    line_wait((nzh - 1) * np_, turn_send_sem)
    for which in range(3):
        if which > 0:
            a2a_drain(which)
        gather_drain(which)
    for copy in halos0 + halos1 + halos2:
        copy.wait_send()


def per_device(fv, sh, link, kel, longwave, shortwave):
    vmem = pl.BlockSpec(memory_space=pltpu.VMEM)
    hbm = pl.BlockSpec(memory_space=pltpu.HBM)
    field = jax.ShapeDtypeStruct((LV, PX, CY), F32)
    np_ = DIMS[0] * DIMS[2] * DIMS[3]
    steps = int(math.log2(NT))
    padded = pltpu.VMEM((LP, PX, CY), F32)
    whole = pltpu.VMEM((LV, PX, CY), F32)
    lines = pltpu.VMEM((NT, 1, LP * PX), F32)
    middle = pltpu.VMEM((DIMS[1], np_, 1, LP * PX), F32)
    turned = pltpu.VMEM((DIMS[0], DIMS[1], DIMS[2] * DIMS[3], 1, LP * PX), F32)
    rims = pltpu.VMEM((3, LV, CY), F32)
    corners = pltpu.VMEM((3, PX, CY), F32)
    dma = pltpu.SemaphoreType.DMA
    return pl.pallas_call(
        kernel,
        out_shape=(field, field),
        in_specs=[hbm] * 6,
        out_specs=(vmem, vmem),
        scratch_shapes=[padded, whole, whole]
        + [pltpu.SMEM((LV - 1,), F32), pltpu.SMEM((LV,), F32), pltpu.SMEM((LV,), F32)]
        + [padded] * 10
        + [lines, middle, turned]
        + [lines] * 4
        + [rims, rims, corners, corners, rims, rims, corners, corners]
        + [
            pltpu.VMEM((3, DIMS[1] * NG, 128), F32),
            pltpu.VMEM((3, np_, NM // 8, 128), F32),
            pltpu.VMEM((steps, NG, GP, NT), F32),
            pltpu.VMEM((steps, NG, GP, NT), F32),
            pltpu.VMEM((NG, GP, NT), F32),
            pltpu.VMEM((NT - 1, 1, LP * PX), F32),
            pltpu.VMEM((DIMS[1] * NG, 1, 128), F32),
            pltpu.VMEM((LV, CY), F32),
            pltpu.VMEM((LV, CY), F32),
            dma,
            dma((DIMS[0],)),
            dma((DIMS[0],)),
            dma,
            dma((6,)),
            dma((3,)),
            dma((3,)),
            dma((3, 4)),
            dma((3, 4)),
            dma((3,)),
            dma((3,)),
            dma((3,)),
            dma((3,)),
        ],
        compiler_params=pltpu.CompilerParams(
            collective_id=0, has_side_effects=True, vmem_limit_bytes=67043328
        ),
        name="step",
    )(fv, sh, kel, link, longwave, shortwave)


def solution(mesh):
    spread = P(None, "tile", "grp")
    columns = P(None, None, ("tile", "grp"))
    return jax.shard_map(
        per_device,
        mesh=mesh,
        in_specs=(spread, spread, P(), columns, P(), P()),
        out_specs=(spread, columns),
        check_vma=False,
    )
```
